32 devices in a mesh: ctx: 4 (over z), dp: 4 (over y, x), section: 2 (over core).
Axes of the slice: x: 2, y: 2, z: 4, core: 2. Of those that a mesh axis runs over, the one named last changes fastest.
Arguments:
- tokens: bfloat16 [2, 4, 512, 4096], P('section', 'dp', 'ctx'), may hold values from -6 to 6
- norm_gain: float32 [2, 4096], P('section'), may hold values from 0.1 to 1.9
- query_weight: bfloat16 [2, 4096, 512], P('section', 'dp'), may hold values from -0.421875 to 0.421875
- key_weight: bfloat16 [2, 4096, 128], P('section', 'dp'), may hold values from -0.421875 to 0.421875
- value_weight: bfloat16 [2, 4096, 128], P('section', 'dp'), may hold values from -0.09375 to 0.09375
- block_order: int32 [2, 4, 8], P('section', 'dp'), may hold values from 0 to 7, each once within a row
- doc_ids: int32 [2, 4, 512], P('section', 'dp'), may hold values from 0 to 3, never falling along the last dimension, each value on 1 to 256 neighbouring positions
Outputs:
- passed: bfloat16 [2, 4, 512, 512], P('section', 'dp', 'ctx')
The draws below stay inside these ranges and needn't reach their ends.
Inputs may be any that keep to these rules, and one draw needn't show every extreme that they name: `block_order`: each row is a permutation of the block numbers. `doc_ids`: never falling along positions; every document holds 1 to 256 positions, and one holds exactly 256.
All inputs are finite; a program needn't handle non-finite values.
Results may differ from the reference program's by a relative error of at most 0.012.
Values may be sent and summed in bfloat16 or wider, within the bound.
No kernel may reach another device: no remote copies, remote signals or barrier semaphores. Data moves between devices by JAX's collectives and lax.ppermute only.
A program may use at most 64 MiB of HBM per device.

```python
import math
import jax
import jax.numpy as jnp
import numpy as np
from jax import lax

D = 4096
HEAD = 128
QH = 4
DOCS = 4
HALF = 64
L = 512
BLOCKS = 8
SECTIONS = 2
SEQS = 4


def draw_query_weight(key, part):
    other = jnp.clip(jax.random.normal(jax.random.fold_in(key, 11), (SECTIONS, D, QH * HEAD), jnp.float32), -6.0, 6.0) / math.sqrt(D)
    return other.astype(jnp.bfloat16)


def draw_key_weight(key, part):
    result = jnp.clip(jax.random.normal(jax.random.fold_in(key, 13), (SECTIONS, D, HEAD), jnp.float32), -6.0, 6.0) / math.sqrt(D)
    return result.astype(jnp.bfloat16)


def draw_tokens(key, part):
    base = jnp.clip(jax.random.normal(jax.random.fold_in(key, 17), (SECTIONS, SEQS, L, D), jnp.float32), -6.0, 6.0)
    return base.astype(jnp.bfloat16)


def block_scale(key, extent, cuts, least, top_value):
    loudness = 1.0
    for position, shards_of in cuts:
        draws = jax.random.uniform(jax.random.fold_in(jax.random.fold_in(key, 6), position), (shards_of,), jnp.float32, least / len(cuts), top_value / len(cuts))
        loudness = loudness * jnp.repeat(jnp.exp(draws), extent[position] // shards_of).reshape((-1,) + (1,) * (len(extent) - 1 - position))
    return loudness


def length_profile(count, total, limit, skew):
    weights = [(1 << 20) // math.isqrt(rank ** skew) + 1 for rank in range(2, count + 1)]
    rest, holding = total - limit - (count - 1), [1] * (count - 1)
    while rest > 0:
        movable = [i for i in range(count - 1) if holding[i] < limit]
        whole, remaining = sum([weights[i] for i in movable]), rest
        for i in movable:
            addition = min(limit - holding[i], max(1, remaining * weights[i] // whole), rest)
            holding[i] = holding[i] + addition
            rest = rest - addition
    return np.array([limit] + holding)


def ragged_sizes(key, count, total, bound, lean):
    if count == 2:
        one = jax.random.randint(key, (), max(1, total - bound), min(bound, total - 1) + 1)
        return jnp.stack([one, total - one])
    tallies = jnp.asarray(length_profile(count, total, bound, lean), jnp.int32)
    pairs = (count - 1) // 2
    source_of, taker = tallies[1:1 + 2 * pairs:2], tallies[2:2 + 2 * pairs:2]
    room = jnp.minimum(source_of - 1, bound - taker)
    passed = jax.random.randint(jax.random.fold_in(key, 1), (pairs,), 0, 1 << 20) % (room + 1)
    tallies = tallies.at[1:1 + 2 * pairs:2].set(source_of - passed).at[2:2 + 2 * pairs:2].set(taker + passed)
    return tallies[jax.random.permutation(jax.random.fold_in(key, 2), count)]


def noise(key, extent, scale, limit, cuts=(), held_as=jnp.bfloat16):
    entries = scale * jax.random.normal(key, extent, jnp.float32)
    if cuts:
        entries = entries * block_scale(key, extent, cuts, -0.22, 0.18)
    return jnp.clip(entries, -limit, limit).astype(held_as)


def setup_inputs(seed: int = 0) -> dict:
    splits = jax.random.split(jax.random.key(seed), 8)
    tokens = draw_tokens(jax.random.fold_in(splits[7], 71), 0)
    norm_gain = jnp.clip(1.0 + 0.18 * jax.random.normal(splits[1], (SECTIONS, D), jnp.float32), 0.1, 1.9)
    query_weight = draw_query_weight(jax.random.fold_in(splits[7], 71), 0)
    key_weight = draw_key_weight(jax.random.fold_in(splits[7], 71), 0)
    value_weight = noise(splits[4], (SECTIONS, D, HEAD), D ** -0.5, 0.09375, ((0, 2), (1, 4)))
    block_order = jax.vmap(lambda own: jax.random.permutation(own, BLOCKS))(jax.random.split(splits[5], SECTIONS * SEQS)).reshape((SECTIONS, SEQS, BLOCKS)).astype(jnp.int32)
    doc_ids = jax.vmap(lambda own: jnp.searchsorted(jnp.cumsum(ragged_sizes(own, DOCS, L, L // 2, 2)), jnp.arange(L), side="right"))(jax.random.split(splits[6], SECTIONS * SEQS)).reshape((SECTIONS, SEQS, L)).astype(jnp.int32)
    return {"tokens": tokens, "norm_gain": norm_gain, "query_weight": query_weight, "key_weight": key_weight, "value_weight": value_weight, "block_order": block_order, "doc_ids": doc_ids}


ROPE_BASE = 500000.0
EPSILON = 1e-05
MASKED = -1e+30

def round_trip(values):
    return lax.optimization_barrier(values.astype(jnp.bfloat16)).astype(jnp.float32)

def rotate_pairs(values, positions, head_size):
    count_rows = values.shape[0]
    shaped = values.reshape(count_rows, -1, head_size)
    halfway = head_size // 2
    freqs = ROPE_BASE ** (-jnp.arange(halfway, dtype=jnp.float32) * 2.0 / head_size)
    angles = positions.astype(jnp.float32)[:, None, None] * freqs[None, None, :]
    cosine = jnp.cos(angles)
    sine = jnp.sin(angles)
    first_half = shaped[..., :halfway]
    second_half = shaped[..., halfway:]
    turned = jnp.concatenate([first_half * cosine - second_half * sine, second_half * cosine + first_half * sine], axis=-1)
    return turned.reshape(count_rows, -1)

def one_sequence(rows, gain_row, query_section, key_section, value_section, order, documents):
    widened = rows.astype(jnp.float32)
    normed = (widened * lax.rsqrt(lax.optimization_barrier(jnp.mean(widened * widened, axis=-1, keepdims=True)) + EPSILON) * gain_row[None, :]).astype(jnp.bfloat16)
    q_raw = jnp.dot(normed, query_section, preferred_element_type=jnp.float32)
    k_raw = jnp.dot(normed, key_section, preferred_element_type=jnp.float32)
    v_raw = jnp.dot(normed, value_section, preferred_element_type=jnp.float32)
    positions = (order[:, None].astype(jnp.int32) * HALF + jnp.arange(HALF, dtype=jnp.int32)[None, :]).reshape(-1)
    row_docs = documents[positions]
    queries = round_trip(rotate_pairs(q_raw, positions, HEAD)).reshape(L, QH, HEAD)
    keys = round_trip(rotate_pairs(k_raw, positions, HEAD))
    values = round_trip(v_raw)
    block = math.gcd(L, 512)

    def one_block(index):
        begin = (index * block).astype(jnp.int32)
        query_block = lax.dynamic_slice_in_dim(queries, begin, block, 0)
        query_pos = lax.dynamic_slice_in_dim(positions, begin, block, 0)
        query_doc = lax.dynamic_slice_in_dim(row_docs, begin, block, 0)
        scores = jnp.einsum('qhd,kd->hqk', query_block, keys) * HEAD ** (-0.5)
        allowed = (row_docs[None, :] == query_doc[:, None]) & (positions[None, :] <= query_pos[:, None])
        scores = jnp.where(allowed[None], scores, MASKED)
        row_max = lax.optimization_barrier(jnp.max(scores, axis=-1))
        probs = jnp.where(allowed[None], jnp.exp(scores - row_max[..., None]), 0.0)
        total = lax.optimization_barrier(jnp.sum(probs, axis=-1))
        numer = jnp.einsum('hqk,kd->hqd', round_trip(probs), values)
        result = numer / total[..., None]
        return result.transpose(1, 0, 2).reshape(block, QH * HEAD).astype(jnp.bfloat16)
    blocks = lax.map(one_block, jnp.arange(L // block, dtype=jnp.int32))
    return blocks.reshape(L, QH * HEAD)

def reference(tokens, norm_gain, query_weight, key_weight, value_weight, block_order, doc_ids):
    section_outputs = []
    for section in range(SECTIONS):
        sequence_outputs = []
        for sequence in range(SEQS):
            sequence_outputs.append(one_sequence(tokens[section, sequence], norm_gain[section], query_weight[section], key_weight[section], value_weight[section], block_order[section, sequence], doc_ids[section, sequence]))
        section_outputs.append(jnp.stack(sequence_outputs))
    attended = jnp.stack(section_outputs)
    return jnp.roll(attended, 1, axis=0)
```

```python
import functools

import jax
import jax.numpy as jnp
from jax import lax
from jax.experimental import pallas as pl
from jax.experimental.pallas import tpu as pltpu
from jax.sharding import PartitionSpec as P

ROPE_BASE = 500000.0
EPSILON = 1e-05
MASKED = -1e30
DIRECT = 8


def partner(index, step, count):
    if count & (count - 1) == 0:
        return index ^ step
    return (step - index) % count


def swap_dp(x, step, count):
    return lax.ppermute(x, "dp", [(i, partner(i, step, count)) for i in range(count)])


def to_next_section(x, step, count, sections):
    moves = [
        (i * sections + s, partner(i, step, count) * sections + (s + 1) % sections)
        for i in range(count)
        for s in range(sections)
    ]
    return lax.ppermute(x, ("dp", "section"), moves)


def cut_kernel(count, slots_ref, rows_ref, gain_ref, *out_refs):
    wide = rows_ref[...].astype(jnp.float32)
    scale = lax.rsqrt(jnp.mean(wide * wide, axis=-1, keepdims=True) + EPSILON)
    width = out_refs[0].shape[1]
    for k in range(count):
        begin = pl.multiple_of(slots_ref[k] * width, width)
        part = rows_ref[:, pl.ds(begin, width)].astype(jnp.float32)
        gain = gain_ref[:, pl.ds(begin, width)]
        out_refs[k][...] = (part * scale * gain).astype(jnp.bfloat16)


def cut(rows, gain, slots, count):
    height, features = rows.shape
    width = features // count
    return pl.pallas_call(
        functools.partial(cut_kernel, count),
        out_shape=[jax.ShapeDtypeStruct((height, width), jnp.bfloat16)] * count,
        in_specs=[
            pl.BlockSpec(memory_space=pltpu.SMEM),
            pl.BlockSpec(memory_space=pltpu.VMEM),
            pl.BlockSpec(memory_space=pltpu.VMEM),
        ],
        out_specs=[pl.BlockSpec(memory_space=pltpu.VMEM)] * count,
        name="cut",
    )(slots, rows, gain)


def turn(x, cosine, sine):
    half = x.shape[1] // 2
    first, second = x[:, :half], x[:, half:]
    return jnp.concatenate(
        [first * cosine - second * sine, second * cosine + first * sine], axis=1
    )


def attend_kernel(heads, pieces, *refs):
    parts = refs[:-(6 + pieces)]
    kv_refs = refs[len(parts) : len(parts) + pieces]
    cos_ref, sin_ref, qpos_ref, qdoc_ref, keys_ref, out_ref = refs[len(parts) + pieces :]
    size = cos_ref.shape[1] * 2
    cosine, sine = cos_ref[...], sin_ref[...]
    total_q = parts[0][...].astype(jnp.float32)
    for part in parts[1:]:
        total_q = total_q + part[...].astype(jnp.float32)
    allowed = (keys_ref[1:2, :] == qdoc_ref[...]) & (keys_ref[0:1, :] <= qpos_ref[...])
    keys = jnp.concatenate([ref[:, :size] for ref in kv_refs], axis=0)
    values = jnp.concatenate([ref[:, size:] for ref in kv_refs], axis=0)
    for h in range(heads):
        query = turn(total_q[:, h * size : (h + 1) * size], cosine, sine).astype(jnp.bfloat16)
        scores = lax.dot_general(
            query, keys, (((1,), (1,)), ((), ())), preferred_element_type=jnp.float32
        ) * (size ** (-0.5))
        scores = jnp.where(allowed, scores, MASKED)
        top = jnp.max(scores, axis=-1, keepdims=True)
        probs = jnp.exp(scores - top)
        total = jnp.sum(probs, axis=-1, keepdims=True)
        mixed = jnp.dot(probs.astype(jnp.bfloat16), values, preferred_element_type=jnp.float32)
        out_ref[:, h * size : (h + 1) * size] = (mixed / total).astype(jnp.bfloat16)


def attend(parts, kv, cosine, sine, qpos, qdoc, keys_meta):
    rows, width = parts[0].shape
    size = cosine.shape[1] * 2
    args = (*parts, *kv, cosine, sine, qpos, qdoc, keys_meta)
    return pl.pallas_call(
        functools.partial(attend_kernel, width // size, len(kv)),
        out_shape=jax.ShapeDtypeStruct((rows, width), jnp.bfloat16),
        in_specs=[pl.BlockSpec(memory_space=pltpu.VMEM)] * len(args),
        out_specs=pl.BlockSpec(memory_space=pltpu.VMEM),
        name="attend",
    )(*args)


def attend_long(total_q, keys, values, cosine, sine, qpos, qdoc, keys_meta):
    rows, width = total_q.shape
    size = cosine.shape[1] * 2
    heads = width // size
    queries = jnp.stack(
        [turn(total_q[:, h * size : (h + 1) * size], cosine, sine) for h in range(heads)]
    ).astype(jnp.bfloat16)
    length = keys.shape[0]
    chunk = 1024 if length % 1024 == 0 else length

    def absorb(state, piece):
        run_max, run_total, run_acc = state
        key_block, value_block, key_pos, key_doc = piece
        scores = jnp.einsum(
            "hqd,kd->hqk", queries, key_block, preferred_element_type=jnp.float32
        ) * (size ** (-0.5))
        allowed = (key_doc[None, :] == qdoc) & (key_pos[None, :] <= qpos)
        scores = jnp.where(allowed[None], scores, MASKED)
        new_max = jnp.maximum(run_max, jnp.max(scores, axis=-1))
        weights = jnp.where(allowed[None], jnp.exp(scores - new_max[..., None]), 0.0)
        factor = jnp.exp(run_max - new_max)
        new_total = run_total * factor + jnp.sum(weights, axis=-1)
        new_acc = run_acc * factor[..., None] + jnp.einsum(
            "hqk,kd->hqd",
            weights.astype(jnp.bfloat16),
            value_block,
            preferred_element_type=jnp.float32,
        )
        return (new_max, new_total, new_acc), None

    groups = length // chunk
    start = (
        jnp.full((heads, rows), MASKED, jnp.float32),
        jnp.zeros((heads, rows), jnp.float32),
        jnp.zeros((heads, rows, size), jnp.float32),
    )
    (_, total, acc), _ = lax.scan(
        absorb,
        start,
        (
            keys.reshape(groups, chunk, -1),
            values.reshape(groups, chunk, -1),
            keys_meta[0].reshape(groups, chunk),
            keys_meta[1].reshape(groups, chunk),
        ),
    )
    out = (acc / total[..., None]).transpose(1, 0, 2).reshape(rows, width)
    return out.astype(jnp.bfloat16)


def local(
    count, sections, ring, tokens, norm_gain, query_weight, key_weight, value_weight, block_order, doc_ids
):
    rows_here = tokens[0, 0]
    row_count = rows_here.shape[0]
    length = doc_ids.shape[2]
    blocks = block_order.shape[2]
    block_rows = length // blocks
    size = key_weight.shape[2]
    here = lax.axis_index("dp")
    slots = jnp.stack([partner(here, k, count) for k in range(count)]).astype(jnp.int32)
    slabs = cut(rows_here, norm_gain, slots, count)

    own = [k for k in range(count) if all(partner(i, k, count) == i for i in range(count))]
    arrived = [x if k in own else swap_dp(x, k, count) for k, x in enumerate(slabs)]

    order = block_order[0, 0]
    pick = (order[:, None] == jnp.arange(blocks, dtype=jnp.int32)[None, :]).astype(jnp.int32)
    row_docs = jnp.sum(pick[:, :, None] * doc_ids[0, 0].reshape(1, blocks, block_rows), axis=1)
    positions = order[:, None] * block_rows + jnp.arange(block_rows, dtype=jnp.int32)[None, :]
    meta = jnp.stack([positions.reshape(-1), row_docs.reshape(-1)])
    meta = to_next_section(meta, 0, count, sections) if 0 in own else to_next_section_plain(meta, sections)

    kv_weight = jnp.concatenate([key_weight[0], value_weight[0]], axis=1)
    kv_parts, q_parts = [], []
    for k, x in enumerate(arrived):
        part = jnp.dot(x, kv_weight, preferred_element_type=jnp.float32).astype(jnp.bfloat16)
        kv_parts.append(to_next_section(part, k, count, sections))
    for k, x in enumerate(arrived):
        part = jnp.dot(x, query_weight[0], preferred_element_type=jnp.float32).astype(jnp.bfloat16)
        q_parts.append(to_next_section(part, k, count, sections))

    at = lax.axis_index("ctx")
    mine = lax.dynamic_slice_in_dim(meta, at * row_count, row_count, axis=1)
    qpos, qdoc = mine[0][:, None], mine[1][:, None]
    half = size // 2
    freqs = ROPE_BASE ** (-jnp.arange(half, dtype=jnp.float32) * 2.0 / size)
    angles = qpos.astype(jnp.float32) * freqs[None, :]
    cosine, sine = jnp.cos(angles), jnp.sin(angles)

    kv_raw = sum(p.astype(jnp.float32) for p in kv_parts)
    kv = jnp.concatenate([turn(kv_raw[:, :size], cosine, sine), kv_raw[:, size:]], axis=1)
    kv = kv.astype(jnp.bfloat16)
    if ring <= DIRECT:
        pieces, metas = [kv], [mine]
        for j in range(1, ring):
            pieces.append(lax.ppermute(kv, "ctx", [(i, (i + j) % ring) for i in range(ring)]))
            metas.append(
                lax.dynamic_slice_in_dim(meta, (at - j) % ring * row_count, row_count, axis=1)
            )
        out = attend(q_parts, pieces, cosine, sine, qpos, qdoc, jnp.concatenate(metas, axis=1))
    else:
        everything = lax.all_gather(kv, "ctx", axis=0, tiled=True)
        total_q = sum(p.astype(jnp.float32) for p in q_parts)
        out = attend_long(
            total_q, everything[:, :size], everything[:, size:], cosine, sine, qpos, qdoc, meta
        )
    return out[None, None]


def to_next_section_plain(x, sections):
    return lax.ppermute(x, "section", [(i, (i + 1) % sections) for i in range(sections)])


def solution(mesh):
    in_specs = (
        P("section", "dp", "ctx", None),
        P("section", None),
        P("section", "dp", None),
        P("section", "dp", None),
        P("section", "dp", None),
        P("section", "dp", None),
        P("section", "dp", None),
    )
    out_specs = P("section", "dp", "ctx", None)
    body = functools.partial(
        local, mesh.shape["dp"], mesh.shape["section"], mesh.shape["ctx"]
    )
    return jax.shard_map(body, mesh=mesh, in_specs=in_specs, out_specs=out_specs, check_vma=False)
```

```python
import functools

import jax
import jax.numpy as jnp
from jax import lax
from jax.experimental import pallas as pl
from jax.experimental.pallas import tpu as pltpu
from jax.sharding import PartitionSpec as P

ROPE_BASE = 500000.0
EPSILON = 1e-05
MASKED = -1e30
LOG2E = 1.4426950408889634
DIRECT = 8
GRANT = 8 << 20


def partner(index, step, count):
    if count & (count - 1) == 0:
        return index ^ step
    return (step - index) % count


def swap_dp(x, step, count):
    return lax.ppermute(x, "dp", [(i, partner(i, step, count)) for i in range(count)])


def to_next_section(x, step, count, sections):
    moves = [
        (i * sections + s, partner(i, step, count) * sections + (s + 1) % sections)
        for i in range(count)
        for s in range(sections)
    ]
    return lax.ppermute(x, ("dp", "section"), moves)


def shift_ctx(x, by, ring):
    return lax.ppermute(x, "ctx", [(i, (i + by) % ring) for i in range(ring)])


def local_call(kernel, out_shape, args, in_spaces, scratch=()):
    return pl.pallas_call(
        kernel,
        out_shape=out_shape,
        in_specs=[pl.BlockSpec(memory_space=s) for s in in_spaces],
        out_specs=jax.tree.map(
            lambda s: pl.BlockSpec(memory_space=pltpu.VMEM), out_shape
        ),
        scratch_shapes=scratch,
        compiler_params=pltpu.CompilerParams(vmem_limit_bytes=GRANT),
    )(*args)


def cut_kernel(count, slots_ref, rows_ref, *refs):
    out_refs, sem = refs[:count], refs[count]
    width = out_refs[0].shape[1]
    copies = []
    for k in range(count):
        begin = pl.multiple_of(slots_ref[k] * width, width)
        copies.append(
            pltpu.make_async_copy(rows_ref.at[:, pl.ds(begin, width)], out_refs[k], sem.at[k])
        )
    for copy in copies:
        copy.start()
    for copy in copies:
        copy.wait()


def cut(rows, slots, count):
    height, features = rows.shape
    shape = jax.ShapeDtypeStruct((height, features // count), jnp.bfloat16)
    return local_call(
        functools.partial(cut_kernel, count),
        [shape] * count,
        (slots, rows),
        (pltpu.SMEM, pl.ANY),
        [pltpu.SemaphoreType.DMA((count,))],
    )


def column(row):
    size = row.shape[1]
    down = lax.broadcasted_iota(jnp.int32, (size, size), 0)
    across = lax.broadcasted_iota(jnp.int32, (size, size), 1)
    return jnp.sum(jnp.where(down == across, row, 0.0), axis=1, keepdims=True)


def tables_kernel(length, at_ref, meta_ref, freq_ref, kcos, ksin, qcos, qsin, level, bias):
    rows, size = kcos.shape
    begin = pl.multiple_of(at_ref[0] * rows, rows)
    qpos = column(meta_ref[:, pl.ds(begin, rows)])
    qdoc = column(meta_ref[:, pl.ds(length + begin, rows)])
    scale = column(meta_ref[:, 2 * length :])
    angles = qpos * freq_ref[...]
    sign = jnp.where(lax.broadcasted_iota(jnp.int32, (1, size), 1) < size // 2, -1.0, 1.0)
    cosine, sine = jnp.cos(angles) * scale, jnp.sin(angles) * sign * scale
    kcos[...], ksin[...] = cosine, sine
    more = size ** (-0.5) * LOG2E
    qcos[...], qsin[...] = cosine * more, sine * more
    level[...] = jnp.broadcast_to(scale, level.shape)
    allowed = (meta_ref[:, length : 2 * length] == qdoc) & (meta_ref[:, :length] <= qpos)
    bias[...] = jnp.where(allowed, 0.0, MASKED)


def tables(at, meta, freqs, rows, size, length):
    square = jax.ShapeDtypeStruct((rows, size), jnp.float32)
    return local_call(
        functools.partial(tables_kernel, length),
        [square] * 5 + [jax.ShapeDtypeStruct((rows, length), jnp.float32)],
        (at, meta, freqs),
        (pltpu.SMEM, pltpu.VMEM, pltpu.VMEM),
    )


def summed(refs, start, stop):
    total = refs[0][:, start:stop].astype(jnp.float32)
    for ref in refs[1:]:
        total = total + ref[:, start:stop].astype(jnp.float32)
    return total


def turn(x, cosine, sine):
    return x * cosine + pltpu.roll(x, x.shape[1] // 2, 1) * sine


def mix_kernel(*refs):
    parts, (kcos, ksin, level, out_ref) = refs[:-4], refs[-4:]
    size = kcos.shape[1]
    keys = turn(summed(parts, 0, size), kcos[...], ksin[...])
    out_ref[:, :size] = keys.astype(jnp.bfloat16)
    out_ref[:, size:] = (summed(parts, size, 2 * size) * level[...]).astype(jnp.bfloat16)


def mix(parts, kcos, ksin, level):
    args = (*parts, kcos, ksin, level)
    return local_call(
        mix_kernel,
        jax.ShapeDtypeStruct(parts[0].shape, jnp.bfloat16),
        args,
        [pltpu.VMEM] * len(args),
    )


def attend_kernel(count, ring, at_ref, *refs):
    parts, kv_refs = refs[:count], refs[count : count + ring]
    qcos, qsin, bias, out_ref = refs[count + ring :]
    rows, size = qcos.shape
    keys = jnp.concatenate([ref[:, :size] for ref in kv_refs], axis=0)
    values = jnp.concatenate([ref[:, size:] for ref in kv_refs], axis=0)
    here = [
        pl.multiple_of(lax.rem(at_ref[0] - j + ring, ring) * rows, rows) for j in range(ring)
    ]
    masks = jnp.concatenate([bias[:, pl.ds(b, rows)] for b in here], axis=1)
    for h in range(out_ref.shape[1] // size):
        query = turn(summed(parts, h * size, (h + 1) * size), qcos[...], qsin[...])
        scores = lax.dot_general(
            query.astype(jnp.bfloat16),
            keys,
            (((1,), (1,)), ((), ())),
            preferred_element_type=jnp.float32,
        )
        scores = scores + masks
        probs = jnp.exp2(scores - jnp.max(scores, axis=-1, keepdims=True))
        total = jnp.sum(probs, axis=-1, keepdims=True)
        mixed = jnp.dot(probs.astype(jnp.bfloat16), values, preferred_element_type=jnp.float32)
        out_ref[:, h * size : (h + 1) * size] = (mixed / total).astype(jnp.bfloat16)


def attend(at, parts, kv, qcos, qsin, bias):
    args = (at, *parts, *kv, qcos, qsin, bias)
    return local_call(
        functools.partial(attend_kernel, len(parts), len(kv)),
        jax.ShapeDtypeStruct(parts[0].shape, jnp.bfloat16),
        args,
        [pltpu.SMEM] + [pltpu.VMEM] * (len(args) - 1),
    )


def attend_long(parts, everything, qcos, qsin, bias):
    rows, width = parts[0].shape
    size = qcos.shape[1]
    heads = width // size
    total_q = sum(p.astype(jnp.float32) for p in parts).reshape(rows, heads, size)
    turned = jnp.concatenate([total_q[..., size // 2 :], total_q[..., : size // 2]], axis=-1)
    queries = (total_q * qcos[:, None] + turned * qsin[:, None]).astype(jnp.bfloat16)
    length = everything.shape[0]
    chunk = 1024 if length % 1024 == 0 else length

    def absorb(state, piece):
        run_max, run_total, run_acc = state
        block, mask = piece
        scores = jnp.einsum(
            "qhd,kd->hqk", queries, block[:, :size], preferred_element_type=jnp.float32
        )
        scores = scores + mask[None]
        new_max = jnp.maximum(run_max, jnp.max(scores, axis=-1))
        weights = jnp.where(mask[None] == 0.0, jnp.exp2(scores - new_max[..., None]), 0.0)
        factor = jnp.exp2(run_max - new_max)
        new_total = run_total * factor + jnp.sum(weights, axis=-1)
        new_acc = run_acc * factor[..., None] + jnp.einsum(
            "hqk,kd->hqd",
            weights.astype(jnp.bfloat16),
            block[:, size:],
            preferred_element_type=jnp.float32,
        )
        return (new_max, new_total, new_acc), None

    groups = length // chunk
    start = (
        jnp.full((heads, rows), MASKED, jnp.float32),
        jnp.zeros((heads, rows), jnp.float32),
        jnp.zeros((heads, rows, size), jnp.float32),
    )
    (_, total, acc), _ = lax.scan(
        absorb,
        start,
        (
            everything.reshape(groups, chunk, -1),
            bias.reshape(rows, groups, chunk).transpose(1, 0, 2),
        ),
    )
    out = (acc / total[..., None]).transpose(1, 0, 2).reshape(rows, width)
    return out.astype(jnp.bfloat16)


def local(
    count, sections, ring, tokens, norm_gain, query_weight, key_weight, value_weight, block_order, doc_ids
):
    rows_here = tokens[0, 0]
    row_count = rows_here.shape[0]
    length = doc_ids.shape[2]
    blocks = block_order.shape[2]
    block_rows = length // blocks
    size = key_weight.shape[2]
    depth = key_weight.shape[1]
    here, at = lax.axis_index("dp"), lax.axis_index("ctx").astype(jnp.int32)[None]
    sequence = list(range(count - 1, -1, -1))
    sequence = [sequence[0], *sequence[-2:0:-1], sequence[-1]]
    slots = jnp.stack([partner(here, k, count) for k in sequence]).astype(jnp.int32)
    slabs = cut(rows_here, slots, count)

    arrived = {}
    for k, slab in zip(sequence, slabs):
        arrived[k] = swap_dp(slab, k, count) if k else slab

    wide = rows_here.astype(jnp.float32)
    scale = lax.rsqrt(jnp.mean(wide * wide, axis=-1) + EPSILON)
    order = block_order[0, 0]
    pick = (order[:, None] == jnp.arange(blocks, dtype=jnp.int32)[None, :]).astype(jnp.int32)
    row_docs = jnp.sum(pick[:, :, None] * doc_ids[0, 0].reshape(1, blocks, block_rows), axis=1)
    positions = order[:, None] * block_rows + jnp.arange(block_rows, dtype=jnp.int32)[None, :]
    meta = jnp.concatenate(
        [
            positions.reshape(1, -1).astype(jnp.float32),
            row_docs.reshape(1, -1).astype(jnp.float32),
            scale[None],
        ],
        axis=1,
    )
    meta = lax.ppermute(meta, "section", [(i, (i + 1) % sections) for i in range(sections)])

    half = size // 2
    freqs = ROPE_BASE ** (-jnp.arange(half, dtype=jnp.float32) * 2.0 / size)
    freqs = jnp.concatenate([freqs, freqs])[None]
    kcos, ksin, qcos, qsin, level, bias = tables(at, meta, freqs, row_count, size, length)

    gain = lax.dynamic_slice_in_dim(norm_gain[0], here * depth, depth)[:, None]
    kv_weight = jnp.concatenate([key_weight[0], value_weight[0]], axis=1)
    kv_weight = (kv_weight.astype(jnp.float32) * gain).astype(jnp.bfloat16)
    q_weight = (query_weight[0].astype(jnp.float32) * gain).astype(jnp.bfloat16)

    kv_parts, q_parts = [], []
    last = [sequence[-1], *sequence[:-1]]
    for k in last:
        part = jnp.dot(arrived[k], kv_weight, preferred_element_type=jnp.float32)
        kv_parts.append(to_next_section(part.astype(jnp.bfloat16), k, count, sections))
    for k in last:
        part = jnp.dot(arrived[k], q_weight, preferred_element_type=jnp.float32)
        q_parts.append(to_next_section(part.astype(jnp.bfloat16), k, count, sections))

    kv = mix(kv_parts, kcos, ksin, level)
    if ring <= DIRECT:
        pieces = [kv]
        for j in range(1, ring):
            pieces.append(shift_ctx(kv, j, ring))
        out = attend(at, q_parts, pieces, qcos, qsin, bias)
    else:
        everything = lax.all_gather(kv, "ctx", axis=0, tiled=True)
        out = attend_long(q_parts, everything, qcos, qsin, bias)
    return out[None, None]


def solution(mesh):
    in_specs = (
        P("section", "dp", "ctx", None),
        P("section", None),
        P("section", "dp", None),
        P("section", "dp", None),
        P("section", "dp", None),
        P("section", "dp", None),
        P("section", "dp", None),
    )
    out_specs = P("section", "dp", "ctx", None)

    def body(*args):
        return local(mesh.shape["dp"], mesh.shape["section"], mesh.shape["ctx"], *args)

    return jax.shard_map(body, mesh=mesh, in_specs=in_specs, out_specs=out_specs, check_vma=False)
```

```python
import functools

import jax
import jax.numpy as jnp
import numpy as np
from jax import lax
from jax.experimental import pallas as pl
from jax.experimental.pallas import tpu as pltpu
from jax.sharding import PartitionSpec as P

ROPE_BASE = 500000.0
EPSILON = 1e-05
MASKED = -1e30
LOG2E = 1.4426950408889634
DIRECT = 8
DOCS = 4
GRANT = 8 << 20


def partner(index, step, count):
    if count & (count - 1) == 0:
        return index ^ step
    return (step - index) % count


def swap_dp(x, step, count):
    return lax.ppermute(x, "dp", [(i, partner(i, step, count)) for i in range(count)])


def to_next_section(x, step, count, sections):
    moves = [
        (i * sections + s, partner(i, step, count) * sections + (s + 1) % sections)
        for i in range(count)
        for s in range(sections)
    ]
    return lax.ppermute(x, ("dp", "section"), moves)


def shift_ctx(x, by, ring):
    return lax.ppermute(x, "ctx", [(i, (i + by) % ring) for i in range(ring)])


def on_chip(shape, dtype):
    return pltpu.VMEM(shape, dtype)


def local_call(kernel, out_shape, args, in_specs, **more):
    in_specs = [s if isinstance(s, pl.BlockSpec) else pl.BlockSpec(memory_space=s) for s in in_specs]
    if "out_specs" not in more:
        whole = pl.BlockSpec(memory_space=pltpu.VMEM)
        more["out_specs"] = [whole] * len(out_shape) if isinstance(out_shape, list) else whole
    return pl.pallas_call(
        kernel,
        out_shape=out_shape,
        in_specs=in_specs,
        compiler_params=pltpu.CompilerParams(vmem_limit_bytes=GRANT),
        **more,
    )(*args)


def cut_kernel(count, sequence, here_ref, rows_ref, *refs):
    out_refs, sem = refs[:count], refs[count]
    width = out_refs[0].shape[1]
    copies = []
    for slot, k in enumerate(sequence):
        begin = pl.multiple_of(partner(here_ref[0], k, count) * width, width)
        copies.append(
            pltpu.make_async_copy(
                rows_ref.at[:, pl.ds(begin, width)], out_refs[slot], sem.at[slot]
            )
        )
    for copy in copies:
        copy.start()
    for copy in copies:
        copy.wait()


def cut(rows, here, count, sequence):
    height, features = rows.shape
    rows = pltpu.with_memory_space_constraint(rows, pltpu.HBM)
    return local_call(
        functools.partial(cut_kernel, count, sequence),
        [on_chip((height, features // count), jnp.bfloat16)] * count,
        (here, rows),
        (pltpu.SMEM, pltpu.HBM),
        scratch_shapes=[pltpu.SemaphoreType.DMA((count,))],
    )


def meta_kernel(docs_count, blocks, rows_ref, order_ref, docs_ref, out_ref):
    height = rows_ref.shape[0]
    length = docs_ref.shape[1]
    block_rows = length // blocks
    squares = jnp.zeros((height, 128), jnp.float32)
    for i in range(rows_ref.shape[1] // 128):
        part = rows_ref[:, i * 128 : (i + 1) * 128].astype(jnp.float32)
        squares = squares + part * part
    mean = jnp.sum(squares, axis=1, keepdims=True) / rows_ref.shape[1]
    scale = lax.rsqrt(mean + EPSILON)
    down = lax.broadcasted_iota(jnp.int32, (height, height), 0)
    across = lax.broadcasted_iota(jnp.int32, (height, height), 1)
    out_ref[:, 2 * length :] = jnp.sum(
        jnp.where(down == across, scale, 0.0), axis=0, keepdims=True
    )
    lane = lax.broadcasted_iota(jnp.int32, (1, length), 1)
    block = jnp.zeros((1, length), jnp.int32)
    for b in range(blocks):
        inside = (lane >= b * block_rows) & (lane < (b + 1) * block_rows)
        block = jnp.where(inside, order_ref[0, b] * block_rows - b * block_rows, block)
    positions = (block + lane).astype(jnp.float32)
    number = jnp.zeros((1, length), jnp.float32)
    for d in range(1, docs_count):
        start = jnp.sum((docs_ref[...] < d).astype(jnp.float32), axis=1, keepdims=True)
        number = number + (positions >= start).astype(jnp.float32)
    out_ref[:, :length] = positions
    out_ref[:, length : 2 * length] = number


def describe(rows, order, docs):
    height, length, blocks = rows.shape[0], docs.shape[1], order.shape[1]
    rows = pltpu.with_memory_space_constraint(rows, pltpu.HBM)
    return local_call(
        functools.partial(meta_kernel, DOCS, blocks),
        on_chip((1, 2 * length + height), jnp.float32),
        (rows, order, docs),
        (pltpu.VMEM, pltpu.SMEM, pltpu.VMEM),
    )


def describe_long(rows, order, docs):
    length, blocks = docs.shape[1], order.shape[1]
    wide = rows.astype(jnp.float32)
    scale = lax.rsqrt(jnp.mean(wide * wide, axis=-1) + EPSILON)
    within = jnp.arange(length // blocks, dtype=jnp.int32)
    positions = (order[0][:, None] * (length // blocks) + within[None, :]).reshape(-1)
    number = sum(
        (positions >= jnp.sum((docs[0] < d).astype(jnp.int32))).astype(jnp.float32)
        for d in range(1, DOCS)
    )
    return jnp.concatenate([positions.astype(jnp.float32), number, scale])[None]


def column(row):
    size = row.shape[1]
    down = lax.broadcasted_iota(jnp.int32, (size, size), 0)
    across = lax.broadcasted_iota(jnp.int32, (size, size), 1)
    return jnp.sum(jnp.where(down == across, row, 0.0), axis=1, keepdims=True)


def tables_kernel(length, at_ref, meta_ref, freq_ref, kcos, ksin, qcos, qsin, level, bias):
    rows, size = kcos.shape
    begin = pl.multiple_of(at_ref[0] * rows, rows)
    qpos = column(meta_ref[:, pl.ds(begin, rows)])
    qdoc = column(meta_ref[:, pl.ds(length + begin, rows)])
    scale = column(meta_ref[:, 2 * length :])
    angles = qpos * freq_ref[...]
    sign = jnp.where(lax.broadcasted_iota(jnp.int32, (1, size), 1) < size // 2, -1.0, 1.0)
    cosine, sine = jnp.cos(angles) * scale, jnp.sin(angles) * sign * scale
    kcos[...], ksin[...] = cosine, sine
    more = size ** (-0.5) * LOG2E
    qcos[...], qsin[...] = cosine * more, sine * more
    level[...] = jnp.broadcast_to(scale, level.shape)
    allowed = (meta_ref[:, length : 2 * length] == qdoc) & (meta_ref[:, :length] <= qpos)
    bias[...] = jnp.where(allowed, 0.0, MASKED)


def tables(at, meta, freqs, rows, size, length):
    square = on_chip((rows, size), jnp.float32)
    return local_call(
        functools.partial(tables_kernel, length),
        [square] * 5 + [on_chip((rows, length), jnp.float32)],
        (at, meta, freqs),
        (pltpu.SMEM, pltpu.VMEM, pltpu.VMEM),
    )


def scale_kernel(here_ref, gain_ref, query_ref, key_ref, value_ref, kv_out, q_out):
    rows, size = key_ref.shape
    step = pl.program_id(0)
    for i in range(rows // size):
        begin = ((here_ref[0] * pl.num_programs(0) + step) * (rows // size) + i) * size
        gain = column(gain_ref[:, pl.ds(pl.multiple_of(begin, size), size)])
        part = slice(i * size, (i + 1) * size)
        target = pl.ds(pl.multiple_of(step * rows + i * size, size), size)
        kv_out[target, :size] = (key_ref[part, :].astype(jnp.float32) * gain).astype(jnp.bfloat16)
        kv_out[target, size:] = (value_ref[part, :].astype(jnp.float32) * gain).astype(jnp.bfloat16)
        q_out[target, :] = (query_ref[part, :].astype(jnp.float32) * gain).astype(jnp.bfloat16)


def scale_weights(here, gain, query_weight, key_weight, value_weight):
    depth, size = key_weight.shape
    width = query_weight.shape[1]
    steps = 4
    rows = depth // steps
    held = [pltpu.with_memory_space_constraint(w, pltpu.HBM) for w in (query_weight, key_weight, value_weight)]
    return local_call(
        scale_kernel,
        [on_chip((depth, 2 * size), jnp.bfloat16), on_chip((depth, width), jnp.bfloat16)],
        (here, gain, *held),
        [
            pltpu.SMEM,
            pltpu.VMEM,
            pl.BlockSpec((rows, width), lambda i: (i, 0)),
            pl.BlockSpec((rows, size), lambda i: (i, 0)),
            pl.BlockSpec((rows, size), lambda i: (i, 0)),
        ],
        grid=(steps,),
    )


def dot_kernel(x_ref, w_ref, out_ref):
    out_ref[...] = jnp.dot(
        x_ref[...], w_ref[...], preferred_element_type=jnp.float32
    ).astype(jnp.bfloat16)


def project(x, weight):
    return local_call(
        dot_kernel,
        on_chip((x.shape[0], weight.shape[1]), jnp.bfloat16),
        (x, weight),
        [pltpu.VMEM] * 2,
    )


def summed(refs, start, stop):
    total = refs[0][:, start:stop].astype(jnp.float32)
    for ref in refs[1:]:
        total = total + ref[:, start:stop].astype(jnp.float32)
    return total


def turn(x, cosine, sine):
    return x * cosine + pltpu.roll(x, x.shape[1] // 2, 1) * sine


def mix_kernel(*refs):
    parts, (kcos, ksin, level, out_ref) = refs[:-4], refs[-4:]
    size = kcos.shape[1]
    keys = turn(summed(parts, 0, size), kcos[...], ksin[...])
    out_ref[:, :size] = keys.astype(jnp.bfloat16)
    out_ref[:, size:] = (summed(parts, size, 2 * size) * level[...]).astype(jnp.bfloat16)


def mix(parts, kcos, ksin, level):
    args = (*parts, kcos, ksin, level)
    return local_call(
        mix_kernel, on_chip(parts[0].shape, jnp.bfloat16), args, [pltpu.VMEM] * len(args)
    )


def attend_kernel(count, ring, at_ref, *refs):
    parts, kv_refs = refs[:count], refs[count : count + ring]
    qcos, qsin, bias, out_ref = refs[count + ring :]
    rows, size = qcos.shape
    keys = jnp.concatenate([ref[:, :size] for ref in kv_refs], axis=0)
    values = jnp.concatenate([ref[:, size:] for ref in kv_refs], axis=0)
    here = [
        pl.multiple_of(lax.rem(at_ref[0] - j + ring, ring) * rows, rows) for j in range(ring)
    ]
    masks = jnp.concatenate([bias[:, pl.ds(b, rows)] for b in here], axis=1)
    for h in range(out_ref.shape[1] // size):
        query = turn(summed(parts, h * size, (h + 1) * size), qcos[...], qsin[...])
        scores = lax.dot_general(
            query.astype(jnp.bfloat16),
            keys,
            (((1,), (1,)), ((), ())),
            preferred_element_type=jnp.float32,
        )
        scores = scores + masks
        probs = jnp.exp2(scores - jnp.max(scores, axis=-1, keepdims=True))
        total = jnp.sum(probs, axis=-1, keepdims=True)
        mixed = jnp.dot(probs.astype(jnp.bfloat16), values, preferred_element_type=jnp.float32)
        out_ref[:, h * size : (h + 1) * size] = (mixed / total).astype(jnp.bfloat16)


def attend(at, parts, kv, qcos, qsin, bias):
    args = (at, *parts, *kv, qcos, qsin, bias)
    return local_call(
        functools.partial(attend_kernel, len(parts), len(kv)),
        jax.ShapeDtypeStruct(parts[0].shape, jnp.bfloat16),
        args,
        [pltpu.SMEM] + [pltpu.VMEM] * (len(args) - 1),
    )


def attend_long(parts, everything, qcos, qsin, bias):
    rows, width = parts[0].shape
    size = qcos.shape[1]
    heads = width // size
    total_q = sum(p.astype(jnp.float32) for p in parts).reshape(rows, heads, size)
    turned = jnp.concatenate([total_q[..., size // 2 :], total_q[..., : size // 2]], axis=-1)
    queries = (total_q * qcos[:, None] + turned * qsin[:, None]).astype(jnp.bfloat16)
    length = everything.shape[0]
    chunk = 1024 if length % 1024 == 0 else length

    def absorb(state, piece):
        run_max, run_total, run_acc = state
        block, mask = piece
        scores = jnp.einsum(
            "qhd,kd->hqk", queries, block[:, :size], preferred_element_type=jnp.float32
        )
        scores = scores + mask[None]
        new_max = jnp.maximum(run_max, jnp.max(scores, axis=-1))
        weights = jnp.where(mask[None] == 0.0, jnp.exp2(scores - new_max[..., None]), 0.0)
        factor = jnp.exp2(run_max - new_max)
        new_total = run_total * factor + jnp.sum(weights, axis=-1)
        new_acc = run_acc * factor[..., None] + jnp.einsum(
            "hqk,kd->hqd",
            weights.astype(jnp.bfloat16),
            block[:, size:],
            preferred_element_type=jnp.float32,
        )
        return (new_max, new_total, new_acc), None

    groups = length // chunk
    start = (
        jnp.full((heads, rows), MASKED, jnp.float32),
        jnp.zeros((heads, rows), jnp.float32),
        jnp.zeros((heads, rows, size), jnp.float32),
    )
    (_, total, acc), _ = lax.scan(
        absorb,
        start,
        (
            everything.reshape(groups, chunk, -1),
            bias.reshape(rows, groups, chunk).transpose(1, 0, 2),
        ),
    )
    out = (acc / total[..., None]).transpose(1, 0, 2).reshape(rows, width)
    return out.astype(jnp.bfloat16)


def local(
    count, sections, ring, tokens, norm_gain, query_weight, key_weight, value_weight, block_order, doc_ids
):
    rows_here = tokens[0, 0]
    row_count = rows_here.shape[0]
    length = doc_ids.shape[2]
    size = key_weight.shape[2]
    here = lax.axis_index("dp").astype(jnp.int32)[None]
    at = lax.axis_index("ctx").astype(jnp.int32)[None]
    sequence = [count - 1, *range(1, count - 1), 0]
    slabs = cut(rows_here, here, count, sequence)

    arrived = {}
    for k, slab in zip(sequence, slabs):
        arrived[k] = swap_dp(slab, k, count) if k else slab

    tell = describe if ring <= DIRECT else describe_long
    meta = tell(rows_here, block_order[0], doc_ids[0])
    meta = lax.ppermute(meta, "section", [(i, (i + 1) % sections) for i in range(sections)])

    freqs = ROPE_BASE ** (-np.arange(size // 2, dtype=np.float64) * 2.0 / size)
    freqs = jnp.asarray(np.concatenate([freqs, freqs])[None], jnp.float32)
    kcos, ksin, qcos, qsin, level, bias = tables(at, meta, freqs, row_count, size, length)

    kv_weight, q_weight = scale_weights(
        here, norm_gain, query_weight[0], key_weight[0], value_weight[0]
    )

    kv_parts, q_parts = [], []
    for k in [sequence[-1], *sequence[:-1]]:
        part = project(arrived[k], kv_weight)
        kv_parts.append(to_next_section(part, k, count, sections))
        part = project(arrived[k], q_weight)
        q_parts.append(to_next_section(part, k, count, sections))

    kv = mix(kv_parts, kcos, ksin, level)
    if ring <= DIRECT:
        pieces = [kv]
        for j in range(1, ring):
            pieces.append(shift_ctx(kv, j, ring))
        out = attend(at, q_parts, pieces, qcos, qsin, bias)
    else:
        everything = lax.all_gather(kv, "ctx", axis=0, tiled=True)
        out = attend_long(q_parts, everything, qcos, qsin, bias)
    return out[None, None]


def solution(mesh):
    in_specs = (
        P("section", "dp", "ctx", None),
        P("section", None),
        P("section", "dp", None),
        P("section", "dp", None),
        P("section", "dp", None),
        P("section", "dp", None),
        P("section", "dp", None),
    )
    out_specs = P("section", "dp", "ctx", None)

    def body(*args):
        return local(mesh.shape["dp"], mesh.shape["section"], mesh.shape["ctx"], *args)

    return jax.shard_map(body, mesh=mesh, in_specs=in_specs, out_specs=out_specs, check_vma=False)
```

```python
import functools

import jax
import jax.numpy as jnp
import numpy as np
from jax import lax
from jax.experimental import pallas as pl
from jax.experimental.pallas import tpu as pltpu
from jax.sharding import PartitionSpec as P

ROPE_BASE = 500000.0
EPSILON = 1e-05
MASKED = -1e30
LOG2E = 1.4426950408889634
DIRECT = 8
DOCS = 4
GRANT = 8 << 20


def partner(index, step, count):
    if count & (count - 1) == 0:
        return index ^ step
    return (step - index) % count


def swap_dp(x, step, count):
    return lax.ppermute(x, "dp", [(i, partner(i, step, count)) for i in range(count)])


def to_next_section(x, step, count, sections):
    moves = [
        (i * sections + s, partner(i, step, count) * sections + (s + 1) % sections)
        for i in range(count)
        for s in range(sections)
    ]
    return lax.ppermute(x, ("dp", "section"), moves)


def shift_ctx(x, by, ring):
    return lax.ppermute(x, "ctx", [(i, (i + by) % ring) for i in range(ring)])


def on_chip(shape, dtype):
    return pltpu.VMEM(shape, dtype)


def local_call(kernel, out_shape, args, in_specs, **more):
    in_specs = [s if isinstance(s, pl.BlockSpec) else pl.BlockSpec(memory_space=s) for s in in_specs]
    if "out_specs" not in more:
        whole = pl.BlockSpec(memory_space=pltpu.VMEM)
        more["out_specs"] = [whole] * len(out_shape) if isinstance(out_shape, list) else whole
    return pl.pallas_call(
        kernel,
        out_shape=out_shape,
        in_specs=in_specs,
        compiler_params=pltpu.CompilerParams(vmem_limit_bytes=GRANT),
        **more,
    )(*args)


def in_hbm(*arrays):
    return [pltpu.with_memory_space_constraint(x, pltpu.HBM) for x in arrays]


def cut_kernel(count, sequence, here_ref, rows_ref, gain_ref, *refs):
    out_refs, held, sem = refs[: len(sequence)], refs[-2], refs[-1]
    width = out_refs[0].shape[1]
    begins = [pl.multiple_of(partner(here_ref[0], k, count) * width, width) for k in sequence]
    copies = [
        pltpu.make_async_copy(rows_ref.at[:, pl.ds(b, width)], held.at[i], sem.at[i])
        for i, b in enumerate(begins)
    ]
    for copy in copies:
        copy.start()
    for i, copy in enumerate(copies):
        copy.wait()
        gain = gain_ref[:, pl.ds(begins[i], width)]
        out_refs[i][...] = (held[i].astype(jnp.float32) * gain).astype(jnp.bfloat16)


def cut(rows, gain, here, count, sequence):
    height, features = rows.shape
    width = features // count
    return local_call(
        functools.partial(cut_kernel, count, sequence),
        [on_chip((height, width), jnp.bfloat16)] * len(sequence),
        (here, *in_hbm(rows, gain)),
        (pltpu.SMEM, pltpu.HBM, pltpu.VMEM),
        scratch_shapes=[
            pltpu.VMEM((len(sequence), height, width), jnp.bfloat16),
            pltpu.SemaphoreType.DMA((len(sequence),)),
        ],
    )


def product(x, weight):
    return jnp.dot(x, weight, preferred_element_type=jnp.float32).astype(jnp.bfloat16)


def tell(rows_ref, order_ref, docs_ref, out_ref):
    height = rows_ref.shape[0]
    length, blocks = docs_ref.shape[1], order_ref.shape[1]
    block_rows = length // blocks
    squares = jnp.zeros((height, 128), jnp.float32)
    for i in range(rows_ref.shape[1] // 128):
        part = rows_ref[:, i * 128 : (i + 1) * 128].astype(jnp.float32)
        squares = squares + part * part
    mean = jnp.sum(squares, axis=1, keepdims=True) / rows_ref.shape[1]
    scale = lax.rsqrt(mean + EPSILON)
    down = lax.broadcasted_iota(jnp.int32, (height, height), 0)
    across = lax.broadcasted_iota(jnp.int32, (height, height), 1)
    out_ref[:, 2 * length :] = jnp.sum(
        jnp.where(down == across, scale, 0.0), axis=0, keepdims=True
    )
    lane = lax.broadcasted_iota(jnp.int32, (1, length), 1)
    shift = jnp.zeros((1, length), jnp.int32)
    for b in range(blocks):
        inside = (lane >= b * block_rows) & (lane < (b + 1) * block_rows)
        shift = jnp.where(inside, (order_ref[0, b] - b) * block_rows, shift)
    positions = (shift + lane).astype(jnp.float32)
    number = jnp.zeros((1, length), jnp.float32)
    for d in range(1, DOCS):
        start = jnp.sum((docs_ref[...] < d).astype(jnp.float32), axis=1, keepdims=True)
        number = number + (positions >= start).astype(jnp.float32)
    out_ref[:, :length] = positions
    out_ref[:, length : 2 * length] = number


def prepare_kernel(
    here_ref, rows_hbm, gain_ref, kw_hbm, vw_hbm, qw_hbm, order_ref, docs_ref, *refs
):
    w_out, part_out, rows_ref, sem = refs[0], refs[1], refs[-2], refs[-1]
    copies = [pltpu.make_async_copy(rows_hbm, rows_ref, sem.at[0])]
    offset = 0
    for i, weight in enumerate((kw_hbm, vw_hbm, qw_hbm)):
        place = w_out.at[:, offset : offset + weight.shape[1]]
        copies.append(pltpu.make_async_copy(weight, place, sem.at[1 + i]))
        offset += weight.shape[1]
    for copy in copies:
        copy.start()
    copies[0].wait()
    if len(refs) == 5:
        tell(rows_ref, order_ref, docs_ref, refs[2])
    width = w_out.shape[0]
    begin = pl.multiple_of(here_ref[0] * width, width)
    part = rows_ref[:, pl.ds(begin, width)].astype(jnp.float32) * gain_ref[:, pl.ds(begin, width)]
    for copy in copies[1:]:
        copy.wait()
    part_out[...] = product(part.astype(jnp.bfloat16), w_out[...])


def prepare(here, rows, gain, weights, order, docs, with_meta):
    height, depth = rows.shape[0], weights[0].shape[0]
    width = sum(w.shape[1] for w in weights)
    outs = [on_chip((depth, width), jnp.bfloat16), on_chip((height, width), jnp.bfloat16)]
    if with_meta:
        outs.append(on_chip((1, 2 * docs.shape[1] + height), jnp.float32))
    return local_call(
        prepare_kernel,
        outs,
        (here, *in_hbm(rows, gain, *weights, order, docs)),
        (pltpu.SMEM, pltpu.HBM, pltpu.VMEM, *[pltpu.HBM] * 3, pltpu.SMEM, pltpu.VMEM),
        scratch_shapes=[pltpu.VMEM(rows.shape, jnp.bfloat16), pltpu.SemaphoreType.DMA((4,))],
    )


def describe_long(rows, order, docs):
    length, blocks = docs.shape[1], order.shape[1]
    wide = rows.astype(jnp.float32)
    scale = lax.rsqrt(jnp.mean(wide * wide, axis=-1) + EPSILON)
    within = jnp.arange(length // blocks, dtype=jnp.int32)
    positions = (order[0][:, None] * (length // blocks) + within[None, :]).reshape(-1)
    number = sum(
        (positions >= jnp.sum((docs[0] < d).astype(jnp.int32))).astype(jnp.float32)
        for d in range(1, DOCS)
    )
    return jnp.concatenate([positions.astype(jnp.float32), number, scale])[None]


def column(row):
    size = row.shape[1]
    down = lax.broadcasted_iota(jnp.int32, (size, size), 0)
    across = lax.broadcasted_iota(jnp.int32, (size, size), 1)
    return jnp.sum(jnp.where(down == across, row, 0.0), axis=1, keepdims=True)


def tables_kernel(length, at_ref, meta_ref, kcos, ksin, qcos, qsin, level, bias):
    rows, size = kcos.shape
    begin = pl.multiple_of(at_ref[0] * rows, rows)
    qpos = column(meta_ref[:, pl.ds(begin, rows)])
    qdoc = column(meta_ref[:, pl.ds(length + begin, rows)])
    scale = column(meta_ref[:, 2 * length :])
    lane = lax.broadcasted_iota(jnp.int32, (1, size), 1)
    pair = lax.rem(lane, size // 2).astype(jnp.float32)
    angles = qpos * jnp.exp2(pair * (-2.0 * np.log2(ROPE_BASE) / size))
    sign = jnp.where(lane < size // 2, -1.0, 1.0)
    cosine, sine = jnp.cos(angles) * scale, jnp.sin(angles) * sign * scale
    kcos[...], ksin[...] = cosine, sine
    more = size ** (-0.5) * LOG2E
    qcos[...], qsin[...] = cosine * more, sine * more
    level[...] = jnp.broadcast_to(scale, level.shape)
    allowed = (meta_ref[:, length : 2 * length] == qdoc) & (meta_ref[:, :length] <= qpos)
    bias[...] = jnp.where(allowed, 0.0, MASKED)


def tables(at, meta, rows, size, length):
    square = on_chip((rows, size), jnp.float32)
    return local_call(
        functools.partial(tables_kernel, length),
        [square] * 5 + [on_chip((rows, length), jnp.float32)],
        (at, meta),
        (pltpu.SMEM, pltpu.VMEM),
    )


def dot_kernel(x_ref, w_ref, out_ref):
    out_ref[...] = jnp.dot(
        x_ref[...], w_ref[...], preferred_element_type=jnp.float32
    ).astype(jnp.bfloat16)


def project(x, weight):
    return local_call(
        dot_kernel,
        on_chip((x.shape[0], weight.shape[1]), jnp.bfloat16),
        (x, weight),
        [pltpu.VMEM] * 2,
    )


def summed(refs, start, size):
    total = 0.0
    for ref, offset in refs:
        total = total + ref[:, offset + start : offset + start + size].astype(jnp.float32)
    return total


def turn(x, cosine, sine):
    return x * cosine + pltpu.roll(x, x.shape[1] // 2, 1) * sine


def mix_kernel(*refs):
    parts, (kcos, ksin, level, out_ref) = [(r, 0) for r in refs[:-4]], refs[-4:]
    size = kcos.shape[1]
    keys = turn(summed(parts, 0, size), kcos[...], ksin[...])
    out_ref[:, :size] = keys.astype(jnp.bfloat16)
    out_ref[:, size:] = (summed(parts, size, size) * level[...]).astype(jnp.bfloat16)


def mix(parts, kcos, ksin, level):
    args = (*parts, kcos, ksin, level)
    rows, size = kcos.shape
    return local_call(
        mix_kernel, on_chip((rows, 2 * size), jnp.bfloat16), args, [pltpu.VMEM] * len(args)
    )


def project_kernel(start, stop, x_ref, w_ref, out_ref):
    out_ref[...] = product(x_ref[...], w_ref[:, start:stop])


def project(x, weight, start, stop):
    return local_call(
        functools.partial(project_kernel, start, stop),
        on_chip((x.shape[0], stop - start), jnp.bfloat16),
        (x, weight),
        [pltpu.VMEM] * 2,
    )


def attend_kernel(offsets, ring, at_ref, *refs):
    count = len(offsets)
    parts, kv_refs = list(zip(refs, offsets)), refs[count : count + ring]
    qcos, qsin, bias, out_ref = refs[count + ring :]
    rows, size = qcos.shape
    keys = jnp.concatenate([ref[:, :size] for ref in kv_refs], axis=0)
    values = jnp.concatenate([ref[:, size:] for ref in kv_refs], axis=0)
    here = [
        pl.multiple_of(lax.rem(at_ref[0] - j + ring, ring) * rows, rows) for j in range(ring)
    ]
    masks = jnp.concatenate([bias[:, pl.ds(b, rows)] for b in here], axis=1)
    for h in range(out_ref.shape[1] // size):
        query = turn(summed(parts, h * size, size), qcos[...], qsin[...])
        scores = lax.dot_general(
            query.astype(jnp.bfloat16),
            keys,
            (((1,), (1,)), ((), ())),
            preferred_element_type=jnp.float32,
        )
        scores = scores + masks
        probs = jnp.exp2(scores - jnp.max(scores, axis=-1, keepdims=True))
        total = jnp.sum(probs, axis=-1, keepdims=True)
        mixed = jnp.dot(probs.astype(jnp.bfloat16), values, preferred_element_type=jnp.float32)
        out_ref[:, h * size : (h + 1) * size] = (mixed / total).astype(jnp.bfloat16)


def attend(at, parts, offsets, kv, qcos, qsin, bias):
    args = (at, *parts, *kv, qcos, qsin, bias)
    width = parts[0].shape[1] - offsets[0]
    return local_call(
        functools.partial(attend_kernel, offsets, len(kv)),
        jax.ShapeDtypeStruct((parts[0].shape[0], width), jnp.bfloat16),
        args,
        [pltpu.SMEM] + [pltpu.VMEM] * (len(args) - 1),
    )


def attend_long(parts, offsets, everything, qcos, qsin, bias):
    parts = [p[:, o:] for p, o in zip(parts, offsets)]
    rows, width = parts[0].shape
    size = qcos.shape[1]
    heads = width // size
    total_q = sum(p.astype(jnp.float32) for p in parts).reshape(rows, heads, size)
    turned = jnp.concatenate([total_q[..., size // 2 :], total_q[..., : size // 2]], axis=-1)
    queries = (total_q * qcos[:, None] + turned * qsin[:, None]).astype(jnp.bfloat16)
    length = everything.shape[0]
    chunk = 1024 if length % 1024 == 0 else length

    def absorb(state, piece):
        run_max, run_total, run_acc = state
        block, mask = piece
        scores = jnp.einsum(
            "qhd,kd->hqk", queries, block[:, :size], preferred_element_type=jnp.float32
        )
        scores = scores + mask[None]
        new_max = jnp.maximum(run_max, jnp.max(scores, axis=-1))
        weights = jnp.where(mask[None] == 0.0, jnp.exp2(scores - new_max[..., None]), 0.0)
        factor = jnp.exp2(run_max - new_max)
        new_total = run_total * factor + jnp.sum(weights, axis=-1)
        new_acc = run_acc * factor[..., None] + jnp.einsum(
            "hqk,kd->hqd",
            weights.astype(jnp.bfloat16),
            block[:, size:],
            preferred_element_type=jnp.float32,
        )
        return (new_max, new_total, new_acc), None

    groups = length // chunk
    start = (
        jnp.full((heads, rows), MASKED, jnp.float32),
        jnp.zeros((heads, rows), jnp.float32),
        jnp.zeros((heads, rows, size), jnp.float32),
    )
    (_, total, acc), _ = lax.scan(
        absorb,
        start,
        (
            everything.reshape(groups, chunk, -1),
            bias.reshape(rows, groups, chunk).transpose(1, 0, 2),
        ),
    )
    out = (acc / total[..., None]).transpose(1, 0, 2).reshape(rows, width)
    return out.astype(jnp.bfloat16)


def local(
    count, sections, ring, tokens, norm_gain, query_weight, key_weight, value_weight, block_order, doc_ids
):
    rows_here = tokens[0, 0]
    row_count = rows_here.shape[0]
    length = doc_ids.shape[2]
    size = key_weight.shape[2]
    here = lax.axis_index("dp").astype(jnp.int32)[None]
    at = lax.axis_index("ctx").astype(jnp.int32)[None]
    away = [count - 1, *range(1, count - 1)]
    weights = [key_weight[0], value_weight[0], query_weight[0]]
    slabs = cut(rows_here, norm_gain, here, count, away)
    arrived = {}
    for k, slab in zip(away, slabs):
        arrived[k] = swap_dp(slab, k, count)

    weight, part, *meta = prepare(
        here, rows_here, norm_gain, weights, block_order[0], doc_ids[0], ring <= DIRECT
    )
    parts = [to_next_section(part, 0, count, sections)]
    meta = meta[0] if meta else describe_long(rows_here, block_order[0], doc_ids[0])
    meta = lax.ppermute(meta, "section", [(i, (i + 1) % sections) for i in range(sections)])
    kcos, ksin, qcos, qsin, level, bias = tables(at, meta, row_count, size, length)

    part = project(arrived[away[0]], weight, 0, weight.shape[1])
    parts.append(to_next_section(part, away[0], count, sections))
    kv_parts, q_parts, offsets = list(parts), list(parts), [2 * size, 2 * size]
    for k in away[1:]:
        part = project(arrived[k], weight, 0, 2 * size)
        kv_parts.append(to_next_section(part, k, count, sections))
        part = project(arrived[k], weight, 2 * size, weight.shape[1])
        q_parts.append(to_next_section(part, k, count, sections))
        offsets.append(0)

    kv = mix(kv_parts, kcos, ksin, level)
    if ring <= DIRECT:
        pieces = [kv]
        for j in range(1, ring):
            pieces.append(shift_ctx(kv, j, ring))
        out = attend(at, q_parts, offsets, pieces, qcos, qsin, bias)
    else:
        everything = lax.all_gather(kv, "ctx", axis=0, tiled=True)
        out = attend_long(q_parts, offsets, everything, qcos, qsin, bias)
    return out[None, None]


def solution(mesh):
    in_specs = (
        P("section", "dp", "ctx", None),
        P("section", None),
        P("section", "dp", None),
        P("section", "dp", None),
        P("section", "dp", None),
        P("section", "dp", None),
        P("section", "dp", None),
    )
    out_specs = P("section", "dp", "ctx", None)

    def body(*args):
        return local(mesh.shape["dp"], mesh.shape["section"], mesh.shape["ctx"], *args)

    return jax.shard_map(body, mesh=mesh, in_specs=in_specs, out_specs=out_specs, check_vma=False)
```

```python
import functools

import jax
import jax.numpy as jnp
import numpy as np
from jax import lax
from jax.experimental import pallas as pl
from jax.experimental.pallas import tpu as pltpu
from jax.sharding import PartitionSpec as P

ROPE_BASE = 500000.0
EPSILON = 1e-05
MASKED = -1e30
LOG2E = 1.4426950408889634
DIRECT = 4
DOCS = 4
GRANT = 8 << 20


def partner(index, step, count):
    if count & (count - 1):
        raise ValueError("axis size")
    return index ^ step


def far_first(ring):
    return list(range(ring - 1, 0, -1))


def swap_dp(x, step, count):
    return lax.ppermute(x, "dp", [(i, partner(i, step, count)) for i in range(count)])


def to_next_section(x, step, count, sections):
    moves = [
        (i * sections + s, partner(i, step, count) * sections + (s + 1) % sections)
        for i in range(count)
        for s in range(sections)
    ]
    return lax.ppermute(x, ("dp", "section"), moves)


def swap_ctx(x, step, ring):
    return lax.ppermute(x, "ctx", [(i, partner(i, step, ring)) for i in range(ring)])


def on_chip(shape, dtype):
    return pltpu.VMEM(shape, dtype)


def local_call(kernel, out_shape, args, in_specs, **more):
    in_specs = [s if isinstance(s, pl.BlockSpec) else pl.BlockSpec(memory_space=s) for s in in_specs]
    if "out_specs" not in more:
        whole = pl.BlockSpec(memory_space=pltpu.VMEM)
        more["out_specs"] = [whole] * len(out_shape) if isinstance(out_shape, list) else whole
    return pl.pallas_call(
        kernel,
        out_shape=out_shape,
        in_specs=in_specs,
        compiler_params=pltpu.CompilerParams(vmem_limit_bytes=GRANT),
        **more,
    )(*args)


def in_hbm(*arrays):
    return [pltpu.with_memory_space_constraint(x, pltpu.HBM) for x in arrays]


def cut_kernel(count, sequence, here_ref, rows_ref, *refs):
    out_refs, sem = refs[:-1], refs[-1]
    width = out_refs[0].shape[1]
    copies = []
    for i, k in enumerate(sequence):
        begin = pl.multiple_of(partner(here_ref[0], k, count) * width, width)
        copies.append(
            pltpu.make_async_copy(rows_ref.at[:, pl.ds(begin, width)], out_refs[i], sem.at[i])
        )
    for copy in copies:
        copy.start()
    for copy in copies:
        copy.wait()


def cut(rows, here, count, sequence):
    height, features = rows.shape
    return local_call(
        functools.partial(cut_kernel, count, sequence),
        [on_chip((height, features // count), jnp.bfloat16)] * len(sequence),
        (here, *in_hbm(rows)),
        (pltpu.SMEM, pltpu.HBM),
        scratch_shapes=[pltpu.SemaphoreType.DMA((len(sequence),))],
    )


def product(x, weight):
    return jnp.dot(x, weight, preferred_element_type=jnp.float32).astype(jnp.bfloat16)


def tell(rows_ref, order_ref, docs_ref, out_ref):
    height = rows_ref.shape[0]
    length, blocks = docs_ref.shape[1], order_ref.shape[1]
    block_rows = length // blocks
    squares = jnp.zeros((height, 128), jnp.float32)
    for i in range(rows_ref.shape[1] // 128):
        part = rows_ref[:, i * 128 : (i + 1) * 128].astype(jnp.float32)
        squares = squares + part * part
    mean = jnp.sum(squares, axis=1, keepdims=True) / rows_ref.shape[1]
    scale = lax.rsqrt(mean + EPSILON)
    down = lax.broadcasted_iota(jnp.int32, (height, height), 0)
    across = lax.broadcasted_iota(jnp.int32, (height, height), 1)
    out_ref[:, 2 * length :] = jnp.sum(
        jnp.where(down == across, scale, 0.0), axis=0, keepdims=True
    )
    lane = lax.broadcasted_iota(jnp.int32, (1, length), 1)
    shift = jnp.zeros((1, length), jnp.int32)
    for b in range(blocks):
        inside = (lane >= b * block_rows) & (lane < (b + 1) * block_rows)
        shift = jnp.where(inside, (order_ref[0, b] - b) * block_rows, shift)
    positions = (shift + lane).astype(jnp.float32)
    number = jnp.zeros((1, length), jnp.float32)
    for d in range(1, DOCS):
        start = jnp.sum((docs_ref[...] < d).astype(jnp.float32), axis=1, keepdims=True)
        number = number + (positions >= start).astype(jnp.float32)
    out_ref[:, :length] = positions
    out_ref[:, length : 2 * length] = number


def prepare_kernel(
    here_ref, rows_hbm, gain_ref, kw_hbm, vw_hbm, qw_hbm, order_ref, docs_ref, *refs
):
    w_out, part_out = refs[:2]
    rows_ref, w_ref, sem = refs[-3:]
    half = qw_hbm.shape[1] // 2
    copies, offset = [pltpu.make_async_copy(rows_hbm, rows_ref, sem.at[0])], 0
    sources = (kw_hbm, qw_hbm.at[:, :half], vw_hbm, qw_hbm.at[:, half:])
    for i, weight in enumerate(sources):
        place = w_ref.at[:, offset : offset + weight.shape[1]]
        copies.append(pltpu.make_async_copy(weight, place, sem.at[1 + i]))
        offset += weight.shape[1]
    for copy in copies:
        copy.start()
    copies[0].wait()
    if len(refs) == 6:
        tell(rows_ref, order_ref, docs_ref, refs[2])
    width = w_out.shape[0]
    begin = pl.multiple_of(here_ref[0] * width, width)
    for copy in copies[1:]:
        copy.wait()
    step = 128
    for i in range(0, width, step):
        gain = column(gain_ref[:, pl.ds(pl.multiple_of(begin + i, step), step)])
        scaled = w_ref[i : i + step, :].astype(jnp.float32) * gain
        w_out[i : i + step, :] = scaled.astype(jnp.bfloat16)
    part_out[...] = product(rows_ref[:, pl.ds(begin, width)], w_out[...])


def prepare(here, rows, gain, weights, order, docs, with_meta):
    height, depth = rows.shape[0], weights[0].shape[0]
    width = sum(w.shape[1] for w in weights)
    outs = [on_chip((depth, width), jnp.bfloat16), on_chip((height, width), jnp.bfloat16)]
    if with_meta:
        outs.append(on_chip((1, 2 * docs.shape[1] + height), jnp.float32))
    return local_call(
        prepare_kernel,
        outs,
        (here, *in_hbm(rows, gain, *weights, order, docs)),
        (pltpu.SMEM, pltpu.HBM, pltpu.VMEM, *[pltpu.HBM] * 3, pltpu.SMEM, pltpu.VMEM),
        scratch_shapes=[
            pltpu.VMEM(rows.shape, jnp.bfloat16),
            pltpu.VMEM((depth, width), jnp.bfloat16),
            pltpu.SemaphoreType.DMA((5,)),
        ],
    )


def describe_long(rows, order, docs):
    length, blocks = docs.shape[1], order.shape[1]
    wide = rows.astype(jnp.float32)
    scale = lax.rsqrt(jnp.mean(wide * wide, axis=-1) + EPSILON)
    within = jnp.arange(length // blocks, dtype=jnp.int32)
    positions = (order[0][:, None] * (length // blocks) + within[None, :]).reshape(-1)
    number = sum(
        (positions >= jnp.sum((docs[0] < d).astype(jnp.int32))).astype(jnp.float32)
        for d in range(1, DOCS)
    )
    return jnp.concatenate([positions.astype(jnp.float32), number, scale])[None]


def column(row):
    size = row.shape[1]
    down = lax.broadcasted_iota(jnp.int32, (size, size), 0)
    across = lax.broadcasted_iota(jnp.int32, (size, size), 1)
    return jnp.sum(jnp.where(down == across, row, 0.0), axis=1, keepdims=True)


def tables_kernel(length, at_ref, meta_ref, kcos, ksin, qcos, qsin, level, bias):
    rows, size = kcos.shape
    begin = pl.multiple_of(at_ref[0] * rows, rows)
    qpos = column(meta_ref[:, pl.ds(begin, rows)])
    qdoc = column(meta_ref[:, pl.ds(length + begin, rows)])
    scale = column(meta_ref[:, 2 * length :])
    lane = lax.broadcasted_iota(jnp.int32, (1, size), 1)
    pair = lax.rem(lane, size // 2).astype(jnp.float32)
    angles = qpos * jnp.exp2(pair * (-2.0 * np.log2(ROPE_BASE) / size))
    sign = jnp.where(lane < size // 2, -1.0, 1.0)
    cosine, sine = jnp.cos(angles) * scale, jnp.sin(angles) * sign * scale
    kcos[...], ksin[...] = cosine, sine
    more = size ** (-0.5) * LOG2E
    qcos[...], qsin[...] = cosine * more, sine * more
    level[...] = jnp.broadcast_to(scale, level.shape)
    allowed = (meta_ref[:, length : 2 * length] == qdoc) & (meta_ref[:, :length] <= qpos)
    bias[...] = jnp.where(allowed, 0.0, MASKED)


def tables(at, meta, rows, size, length):
    square = on_chip((rows, size), jnp.float32)
    return local_call(
        functools.partial(tables_kernel, length),
        [square] * 5 + [on_chip((rows, length), jnp.float32)],
        (at, meta),
        (pltpu.SMEM, pltpu.VMEM),
    )


def dot_kernel(x_ref, w_ref, out_ref):
    out_ref[...] = jnp.dot(
        x_ref[...], w_ref[...], preferred_element_type=jnp.float32
    ).astype(jnp.bfloat16)


def project(x, weight):
    return local_call(
        dot_kernel,
        on_chip((x.shape[0], weight.shape[1]), jnp.bfloat16),
        (x, weight),
        [pltpu.VMEM] * 2,
    )


def summed(refs, start, size):
    total = 0.0
    for ref in refs:
        total = total + ref[:, start : start + size].astype(jnp.float32)
    return total


def turn(x, cosine, sine):
    return x * cosine + pltpu.roll(x, x.shape[1] // 2, 1) * sine


def mix_kernel(own_ref, *refs):
    parts, (kcos, ksin, level, out_ref) = refs[:-4], refs[-4:]
    size, half = kcos.shape[1], own_ref.shape[1] // 2
    keys = own_ref[:, :size].astype(jnp.float32) + summed(parts, 0, size)
    values = own_ref[:, half : half + size].astype(jnp.float32) + summed(parts, size, size)
    out_ref[:, :size] = turn(keys, kcos[...], ksin[...]).astype(jnp.bfloat16)
    out_ref[:, size:] = (values * level[...]).astype(jnp.bfloat16)


def mix(own, parts, kcos, ksin, level):
    args = (own, *parts, kcos, ksin, level)
    rows, size = kcos.shape
    return local_call(
        mix_kernel, on_chip((rows, 2 * size), jnp.bfloat16), args, [pltpu.VMEM] * len(args)
    )


def far_kernel(x_ref, w_ref, kv_ref, left_ref, right_ref):
    result = product(x_ref[...], w_ref[...])
    size, half = kv_ref.shape[1] // 2, w_ref.shape[1] // 2
    kv_ref[:, :size] = result[:, :size]
    kv_ref[:, size:] = result[:, half : half + size]
    left_ref[...] = result[:, size:half]
    right_ref[...] = result[:, half + size :]


def far_product(x, weight, size):
    rows, half = x.shape[0], weight.shape[1] // 2
    outs = [on_chip((rows, w), jnp.bfloat16) for w in (2 * size, half - size, half - size)]
    return local_call(far_kernel, outs, (x, weight), [pltpu.VMEM] * 2)


def project_kernel(right, start, size, x_ref, w_ref, *refs):
    half, out_ref = w_ref.shape[1] // 2, refs[-1]
    columns = [w_ref[:, h * half + start : h * half + start + size] for h in (0, 1)]
    both = jnp.dot(
        x_ref[...], jnp.concatenate(columns, axis=1), preferred_element_type=jnp.float32
    )
    for h in (0, 1):
        part = both[:, h * size : (h + 1) * size]
        if len(refs) == 2 and h == right:
            part = part + refs[0][...].astype(jnp.float32)
        out_ref[:, h * size : (h + 1) * size] = part.astype(jnp.bfloat16)


def project(x, weight, more, right, start, size):
    return local_call(
        functools.partial(project_kernel, right, start, size),
        on_chip((x.shape[0], 2 * size), jnp.bfloat16),
        (x, weight, *more),
        [pltpu.VMEM] * (2 + len(more)),
    )


def attend_kernel(count, steps, ring, at_ref, own_ref, *refs):
    parts, kv_refs = refs[:count], refs[count : count + ring]
    qcos, qsin, bias, out_ref = refs[count + ring :]
    rows, size = qcos.shape
    heads = out_ref.shape[1] // size
    keys = jnp.concatenate([ref[:, :size] for ref in kv_refs], axis=0)
    values = jnp.concatenate([ref[:, size:] for ref in kv_refs], axis=0)
    here = [pl.multiple_of(partner(at_ref[0], j, ring) * rows, rows) for j in steps]
    masks = jnp.concatenate([bias[:, pl.ds(b, rows)] for b in here], axis=1)
    for h in range(heads):
        place = own_place(h, heads, size)
        query = own_ref[:, place : place + size].astype(jnp.float32)
        query = turn(query + summed(parts, h * size, size), qcos[...], qsin[...])
        scores = lax.dot_general(
            query.astype(jnp.bfloat16),
            keys,
            (((1,), (1,)), ((), ())),
            preferred_element_type=jnp.float32,
        )
        scores = scores + masks
        probs = jnp.exp2(scores - jnp.max(scores, axis=-1, keepdims=True))
        total = jnp.sum(probs, axis=-1, keepdims=True)
        mixed = jnp.dot(probs.astype(jnp.bfloat16), values, preferred_element_type=jnp.float32)
        out_ref[:, h * size : (h + 1) * size] = (mixed / total).astype(jnp.bfloat16)


def own_place(head, heads, size):
    return (head + (1 if head < heads // 2 else 2)) * size


def attend(at, own, parts, kv, qcos, qsin, bias):
    args = (at, own, *parts, *kv, qcos, qsin, bias)
    steps = [0, *far_first(len(kv))]
    return local_call(
        functools.partial(attend_kernel, len(parts), steps, len(kv)),
        jax.ShapeDtypeStruct(parts[0].shape, jnp.bfloat16),
        args,
        [pltpu.SMEM] + [pltpu.VMEM] * (len(args) - 1),
    )


def attend_long(own, parts, everything, qcos, qsin, bias):
    rows, width = parts[0].shape
    heads, size = width // qcos.shape[1], qcos.shape[1]
    places = [own_place(h, heads, size) for h in range(heads)]
    parts = [*parts, jnp.concatenate([own[:, p : p + size] for p in places], axis=1)]
    size = qcos.shape[1]
    heads = width // size
    total_q = sum(p.astype(jnp.float32) for p in parts).reshape(rows, heads, size)
    turned = jnp.concatenate([total_q[..., size // 2 :], total_q[..., : size // 2]], axis=-1)
    queries = (total_q * qcos[:, None] + turned * qsin[:, None]).astype(jnp.bfloat16)
    length = everything.shape[0]
    chunk = 1024 if length % 1024 == 0 else length

    def absorb(state, piece):
        run_max, run_total, run_acc = state
        block, mask = piece
        scores = jnp.einsum(
            "qhd,kd->hqk", queries, block[:, :size], preferred_element_type=jnp.float32
        )
        scores = scores + mask[None]
        new_max = jnp.maximum(run_max, jnp.max(scores, axis=-1))
        weights = jnp.where(mask[None] == 0.0, jnp.exp2(scores - new_max[..., None]), 0.0)
        factor = jnp.exp2(run_max - new_max)
        new_total = run_total * factor + jnp.sum(weights, axis=-1)
        new_acc = run_acc * factor[..., None] + jnp.einsum(
            "hqk,kd->hqd",
            weights.astype(jnp.bfloat16),
            block[:, size:],
            preferred_element_type=jnp.float32,
        )
        return (new_max, new_total, new_acc), None

    groups = length // chunk
    start = (
        jnp.full((heads, rows), MASKED, jnp.float32),
        jnp.zeros((heads, rows), jnp.float32),
        jnp.zeros((heads, rows, size), jnp.float32),
    )
    (_, total, acc), _ = lax.scan(
        absorb,
        start,
        (
            everything.reshape(groups, chunk, -1),
            bias.reshape(rows, groups, chunk).transpose(1, 0, 2),
        ),
    )
    out = (acc / total[..., None]).transpose(1, 0, 2).reshape(rows, width)
    return out.astype(jnp.bfloat16)


def local(
    count, sections, ring, tokens, norm_gain, query_weight, key_weight, value_weight, block_order, doc_ids
):
    rows_here = tokens[0, 0]
    row_count = rows_here.shape[0]
    length = doc_ids.shape[2]
    size = key_weight.shape[2]
    here = lax.axis_index("dp").astype(jnp.int32)[None]
    at = lax.axis_index("ctx").astype(jnp.int32)[None]
    if count != 4:
        raise ValueError("axis size")
    away = [3, 1, 2]
    weights = [key_weight[0], value_weight[0], query_weight[0]]
    slabs = cut(rows_here, here, count, away)
    arrived = {}
    for k, slab in zip(away, slabs):
        arrived[k] = swap_dp(slab, k, count)

    weight, part, *meta = prepare(
        here, rows_here, norm_gain, weights, block_order[0], doc_ids[0], ring <= DIRECT
    )
    own = to_next_section(part, 0, count, sections)
    meta = meta[0] if meta else describe_long(rows_here, block_order[0], doc_ids[0])
    meta = lax.ppermute(meta, "section", [(i, (i + 1) % sections) for i in range(sections)])
    kcos, ksin, qcos, qsin, level, bias = tables(at, meta, row_count, size, length)

    part, *halves = far_product(arrived[3], weight, size)
    kv_parts = [to_next_section(part, 3, count, sections)]
    relayed = {}
    for k, half in zip((1, 2), halves):
        relayed[3 - k] = swap_dp(half, k, count)

    q_parts = []
    for k in (1, 2):
        right = int(k == 1)
        width = query_weight.shape[2] // 2
        part = project(arrived[k], weight, [], right, 0, size)
        kv_parts.append(to_next_section(part, k, count, sections))
        part = project(arrived[k], weight, [relayed[k]], right, size, width)
        q_parts.append(to_next_section(part, k, count, sections))

    kv = mix(own, kv_parts, kcos, ksin, level)
    if ring <= DIRECT:
        pieces = [kv]
        for j in far_first(ring):
            pieces.append(swap_ctx(kv, j, ring))
        out = attend(at, own, q_parts, pieces, qcos, qsin, bias)
    else:
        everything = lax.all_gather(kv, "ctx", axis=0, tiled=True)
        out = attend_long(own, q_parts, everything, qcos, qsin, bias)
    return out[None, None]


def solution(mesh):
    in_specs = (
        P("section", "dp", "ctx", None),
        P("section", None),
        P("section", "dp", None),
        P("section", "dp", None),
        P("section", "dp", None),
        P("section", "dp", None),
        P("section", "dp", None),
    )
    out_specs = P("section", "dp", "ctx", None)

    def body(*args):
        return local(mesh.shape["dp"], mesh.shape["section"], mesh.shape["ctx"], *args)

    return jax.shard_map(body, mesh=mesh, in_specs=in_specs, out_specs=out_specs, check_vma=False)
```

```python
import functools

import jax
import jax.numpy as jnp
import numpy as np
from jax import lax
from jax.experimental import pallas as pl
from jax.experimental.pallas import tpu as pltpu
from jax.sharding import PartitionSpec as P

ROPE_BASE = 500000.0
EPSILON = 1e-05
MASKED = -1e30
LOG2E = 1.4426950408889634
DIRECT = 4
DOCS = 4
GRANT = 8 << 20


def partner(index, step, count):
    if count & (count - 1):
        raise ValueError("axis size")
    return index ^ step


def far_first(ring):
    return [3, 2, 1] if ring == 4 else list(range(ring - 1, 0, -1))


def swap_dp(x, step, count):
    return lax.ppermute(x, "dp", [(i, partner(i, step, count)) for i in range(count)])


def to_next_section(x, step, count, sections):
    moves = [
        (i * sections + s, partner(i, step, count) * sections + (s + 1) % sections)
        for i in range(count)
        for s in range(sections)
    ]
    return lax.ppermute(x, ("dp", "section"), moves)


def swap_ctx(x, step, ring):
    return lax.ppermute(x, "ctx", [(i, partner(i, step, ring)) for i in range(ring)])


def on_chip(shape, dtype):
    return pltpu.VMEM(shape, dtype)


def local_call(kernel, out_shape, args, in_specs, **more):
    in_specs = [s if isinstance(s, pl.BlockSpec) else pl.BlockSpec(memory_space=s) for s in in_specs]
    if "out_specs" not in more:
        whole = pl.BlockSpec(memory_space=pltpu.VMEM)
        more["out_specs"] = [whole] * len(out_shape) if isinstance(out_shape, list) else whole
    return pl.pallas_call(
        kernel,
        out_shape=out_shape,
        in_specs=in_specs,
        compiler_params=pltpu.CompilerParams(vmem_limit_bytes=GRANT),
        **more,
    )(*args)


def in_hbm(*arrays):
    return [pltpu.with_memory_space_constraint(x, pltpu.HBM) for x in arrays]


def cut_kernel(count, sequence, here_ref, rows_ref, *refs):
    out_refs, sem = refs[:-1], refs[-1]
    width = out_refs[0].shape[1]
    copies = []
    for i, k in enumerate(sequence):
        begin = pl.multiple_of(partner(here_ref[0], k, count) * width, width)
        copies.append(
            pltpu.make_async_copy(rows_ref.at[:, pl.ds(begin, width)], out_refs[i], sem.at[i])
        )
    for copy in copies:
        copy.start()
    for copy in copies:
        copy.wait()


def cut(rows, here, count, sequence):
    height, features = rows.shape
    return local_call(
        functools.partial(cut_kernel, count, sequence),
        [on_chip((height, features // count), jnp.bfloat16)] * len(sequence),
        (here, *in_hbm(rows)),
        (pltpu.SMEM, pltpu.HBM),
        scratch_shapes=[pltpu.SemaphoreType.DMA((len(sequence),))],
    )


def product(x, weight):
    return jnp.dot(x, weight, preferred_element_type=jnp.float32).astype(jnp.bfloat16)


def tell(rows_ref, order_ref, docs_ref, out_ref):
    height = rows_ref.shape[0]
    length, blocks = docs_ref.shape[1], order_ref.shape[1]
    block_rows = length // blocks
    squares = jnp.zeros((height, 128), jnp.float32)
    for i in range(rows_ref.shape[1] // 128):
        part = rows_ref[:, i * 128 : (i + 1) * 128].astype(jnp.float32)
        squares = squares + part * part
    mean = jnp.sum(squares, axis=1, keepdims=True) / rows_ref.shape[1]
    scale = lax.rsqrt(mean + EPSILON)
    down = lax.broadcasted_iota(jnp.int32, (height, height), 0)
    across = lax.broadcasted_iota(jnp.int32, (height, height), 1)
    out_ref[:, 2 * length :] = jnp.sum(
        jnp.where(down == across, scale, 0.0), axis=0, keepdims=True
    )
    lane = lax.broadcasted_iota(jnp.int32, (1, length), 1)
    shift = jnp.zeros((1, length), jnp.int32)
    for b in range(blocks):
        inside = (lane >= b * block_rows) & (lane < (b + 1) * block_rows)
        shift = jnp.where(inside, (order_ref[0, b] - b) * block_rows, shift)
    positions = (shift + lane).astype(jnp.float32)
    number = jnp.zeros((1, length), jnp.float32)
    for d in range(1, DOCS):
        start = jnp.sum((docs_ref[...] < d).astype(jnp.float32), axis=1, keepdims=True)
        number = number + (positions >= start).astype(jnp.float32)
    out_ref[:, :length] = positions
    out_ref[:, length : 2 * length] = number


def prepare_kernel(
    here_ref, rows_hbm, gain_ref, kw_hbm, vw_hbm, qw_hbm, order_ref, docs_ref, *refs
):
    w_out, part_out = refs[:2]
    rows_ref, w_ref, sem = refs[-3:]
    half = qw_hbm.shape[1] // 2
    copies, offset = [pltpu.make_async_copy(rows_hbm, rows_ref, sem.at[0])], 0
    sources = (kw_hbm, qw_hbm.at[:, :half], vw_hbm, qw_hbm.at[:, half:])
    for i, weight in enumerate(sources):
        place = w_ref.at[:, offset : offset + weight.shape[1]]
        copies.append(pltpu.make_async_copy(weight, place, sem.at[1 + i]))
        offset += weight.shape[1]
    for copy in copies:
        copy.start()
    copies[0].wait()
    if len(refs) == 6:
        tell(rows_ref, order_ref, docs_ref, refs[2])
    width = w_out.shape[0]
    begin = pl.multiple_of(here_ref[0] * width, width)
    for copy in copies[1:]:
        copy.wait()
    step = 128
    for i in range(0, width, step):
        gain = column(gain_ref[:, pl.ds(pl.multiple_of(begin + i, step), step)])
        scaled = w_ref[i : i + step, :].astype(jnp.float32) * gain
        w_out[i : i + step, :] = scaled.astype(jnp.bfloat16)
    part_out[...] = product(rows_ref[:, pl.ds(begin, width)], w_out[...])


def prepare(here, rows, gain, weights, order, docs, with_meta):
    height, depth = rows.shape[0], weights[0].shape[0]
    width = sum(w.shape[1] for w in weights)
    outs = [on_chip((depth, width), jnp.bfloat16), on_chip((height, width), jnp.bfloat16)]
    if with_meta:
        outs.append(on_chip((1, 2 * docs.shape[1] + height), jnp.float32))
    return local_call(
        prepare_kernel,
        outs,
        (here, *in_hbm(rows, gain, *weights, order, docs)),
        (pltpu.SMEM, pltpu.HBM, pltpu.VMEM, *[pltpu.HBM] * 3, pltpu.SMEM, pltpu.VMEM),
        scratch_shapes=[
            pltpu.VMEM(rows.shape, jnp.bfloat16),
            pltpu.VMEM((depth, width), jnp.bfloat16),
            pltpu.SemaphoreType.DMA((5,)),
        ],
    )


def describe_long(rows, order, docs):
    length, blocks = docs.shape[1], order.shape[1]
    wide = rows.astype(jnp.float32)
    scale = lax.rsqrt(jnp.mean(wide * wide, axis=-1) + EPSILON)
    within = jnp.arange(length // blocks, dtype=jnp.int32)
    positions = (order[0][:, None] * (length // blocks) + within[None, :]).reshape(-1)
    number = sum(
        (positions >= jnp.sum((docs[0] < d).astype(jnp.int32))).astype(jnp.float32)
        for d in range(1, DOCS)
    )
    return jnp.concatenate([positions.astype(jnp.float32), number, scale])[None]


def column(row):
    size = row.shape[1]
    down = lax.broadcasted_iota(jnp.int32, (size, size), 0)
    across = lax.broadcasted_iota(jnp.int32, (size, size), 1)
    return jnp.sum(jnp.where(down == across, row, 0.0), axis=1, keepdims=True)


def tables_kernel(length, at_ref, meta_ref, kcos, ksin, qcos, qsin, level, bias):
    rows, size = kcos.shape
    begin = pl.multiple_of(at_ref[0] * rows, rows)
    qpos = column(meta_ref[:, pl.ds(begin, rows)])
    qdoc = column(meta_ref[:, pl.ds(length + begin, rows)])
    scale = column(meta_ref[:, 2 * length :])
    lane = lax.broadcasted_iota(jnp.int32, (1, size), 1)
    pair = lax.rem(lane, size // 2).astype(jnp.float32)
    angles = qpos * jnp.exp2(pair * (-2.0 * np.log2(ROPE_BASE) / size))
    sign = jnp.where(lane < size // 2, -1.0, 1.0)
    cosine, sine = jnp.cos(angles) * scale, jnp.sin(angles) * sign * scale
    kcos[...], ksin[...] = cosine, sine
    more = size ** (-0.5) * LOG2E
    qcos[...], qsin[...] = cosine * more, sine * more
    level[...] = jnp.broadcast_to(scale, level.shape)
    allowed = (meta_ref[:, length : 2 * length] == qdoc) & (meta_ref[:, :length] <= qpos)
    bias[...] = jnp.where(allowed, 0.0, MASKED)


def tables(at, meta, rows, size, length):
    square = on_chip((rows, size), jnp.float32)
    return local_call(
        functools.partial(tables_kernel, length),
        [square] * 5 + [on_chip((rows, length), jnp.float32)],
        (at, meta),
        (pltpu.SMEM, pltpu.VMEM),
    )


def dot_kernel(x_ref, w_ref, out_ref):
    out_ref[...] = jnp.dot(
        x_ref[...], w_ref[...], preferred_element_type=jnp.float32
    ).astype(jnp.bfloat16)


def project(x, weight):
    return local_call(
        dot_kernel,
        on_chip((x.shape[0], weight.shape[1]), jnp.bfloat16),
        (x, weight),
        [pltpu.VMEM] * 2,
    )


def summed(refs, start, size):
    total = 0.0
    for ref in refs:
        total = total + ref[:, start : start + size].astype(jnp.float32)
    return total


def turn(x, cosine, sine):
    return x * cosine + pltpu.roll(x, x.shape[1] // 2, 1) * sine


def mix_kernel(own_ref, *refs):
    parts, (kcos, ksin, level, out_ref) = refs[:-4], refs[-4:]
    size, half = kcos.shape[1], own_ref.shape[1] // 2
    keys = own_ref[:, :size].astype(jnp.float32) + summed(parts, 0, size)
    values = own_ref[:, half : half + size].astype(jnp.float32) + summed(parts, size, size)
    out_ref[:, :size] = turn(keys, kcos[...], ksin[...]).astype(jnp.bfloat16)
    out_ref[:, size:] = (values * level[...]).astype(jnp.bfloat16)


def mix(own, parts, kcos, ksin, level):
    args = (own, *parts, kcos, ksin, level)
    rows, size = kcos.shape
    return local_call(
        mix_kernel, on_chip((rows, 2 * size), jnp.bfloat16), args, [pltpu.VMEM] * len(args)
    )


def far_kernel(x_ref, w_ref, kv_ref, left_ref, right_ref):
    result = product(x_ref[...], w_ref[...])
    size, half = kv_ref.shape[1] // 2, w_ref.shape[1] // 2
    kv_ref[:, :size] = result[:, :size]
    kv_ref[:, size:] = result[:, half : half + size]
    left_ref[...] = result[:, size:half]
    right_ref[...] = result[:, half + size :]


def far_product(x, weight, size):
    rows, half = x.shape[0], weight.shape[1] // 2
    outs = [on_chip((rows, w), jnp.bfloat16) for w in (2 * size, half - size, half - size)]
    return local_call(far_kernel, outs, (x, weight), [pltpu.VMEM] * 2)


def project_kernel(right, start, size, x_ref, w_ref, *refs):
    half, out_ref = w_ref.shape[1] // 2, refs[-1]
    columns = [w_ref[:, h * half + start : h * half + start + size] for h in (0, 1)]
    both = jnp.dot(
        x_ref[...], jnp.concatenate(columns, axis=1), preferred_element_type=jnp.float32
    )
    for h in (0, 1):
        part = both[:, h * size : (h + 1) * size]
        if len(refs) == 2 and h == right:
            part = part + refs[0][...].astype(jnp.float32)
        out_ref[:, h * size : (h + 1) * size] = part.astype(jnp.bfloat16)


def project(x, weight, more, right, start, size):
    return local_call(
        functools.partial(project_kernel, right, start, size),
        on_chip((x.shape[0], 2 * size), jnp.bfloat16),
        (x, weight, *more),
        [pltpu.VMEM] * (2 + len(more)),
    )


def attend_kernel(count, steps, ring, at_ref, own_ref, *refs):
    parts, kv_refs = refs[:count], refs[count : count + ring]
    qcos, qsin, bias, out_ref, held, sem = refs[count + ring :]
    rows, size = qcos.shape
    heads = out_ref.shape[1] // size
    keys = jnp.concatenate([ref[:, :size] for ref in kv_refs], axis=0)
    values = jnp.concatenate([ref[:, size:] for ref in kv_refs], axis=0)
    values = jnp.concatenate([values, jnp.ones_like(values)], axis=1)
    here = [pl.multiple_of(partner(at_ref[0], j, ring) * rows, rows) for j in steps]
    masks = jnp.concatenate([bias[:, pl.ds(b, rows)] for b in here], axis=1)
    copies = []
    for h in range(heads):
        place = own_place(h, heads, size)
        query = own_ref[:, place : place + size].astype(jnp.float32)
        query = turn(query + summed(parts, h * size, size), qcos[...], qsin[...])
        scores = lax.dot_general(
            query.astype(jnp.bfloat16),
            keys,
            (((1,), (1,)), ((), ())),
            preferred_element_type=jnp.float32,
        )
        scores = scores + masks
        probs = jnp.exp2(scores - jnp.max(scores, axis=-1, keepdims=True))
        mixed = jnp.dot(probs.astype(jnp.bfloat16), values, preferred_element_type=jnp.float32)
        held[h] = (mixed[:, :size] / mixed[:, size:]).astype(jnp.bfloat16)
        place = out_ref.at[:, h * size : (h + 1) * size]
        copies.append(pltpu.make_async_copy(held.at[h], place, sem.at[h]))
        copies[-1].start()
    for copy in copies:
        copy.wait()


def own_place(head, heads, size):
    return (head + (1 if head < heads // 2 else 2)) * size


def attend(at, own, parts, kv, qcos, qsin, bias):
    args = (at, own, *parts, *kv, qcos, qsin, bias)
    rows, width = parts[0].shape
    heads = width // qcos.shape[1]
    steps = [0, *far_first(len(kv))]
    return local_call(
        functools.partial(attend_kernel, len(parts), steps, len(kv)),
        jax.ShapeDtypeStruct(parts[0].shape, jnp.bfloat16),
        args,
        [pltpu.SMEM] + [pltpu.VMEM] * (len(args) - 1),
        out_specs=pl.BlockSpec(memory_space=pltpu.HBM),
        scratch_shapes=[
            pltpu.VMEM((heads, rows, width // heads), jnp.bfloat16),
            pltpu.SemaphoreType.DMA((heads,)),
        ],
    )


def attend_long(own, parts, everything, qcos, qsin, bias):
    rows, width = parts[0].shape
    heads, size = width // qcos.shape[1], qcos.shape[1]
    places = [own_place(h, heads, size) for h in range(heads)]
    parts = [*parts, jnp.concatenate([own[:, p : p + size] for p in places], axis=1)]
    size = qcos.shape[1]
    heads = width // size
    total_q = sum(p.astype(jnp.float32) for p in parts).reshape(rows, heads, size)
    turned = jnp.concatenate([total_q[..., size // 2 :], total_q[..., : size // 2]], axis=-1)
    queries = (total_q * qcos[:, None] + turned * qsin[:, None]).astype(jnp.bfloat16)
    length = everything.shape[0]
    chunk = 1024 if length % 1024 == 0 else length

    def absorb(state, piece):
        run_max, run_total, run_acc = state
        block, mask = piece
        scores = jnp.einsum(
            "qhd,kd->hqk", queries, block[:, :size], preferred_element_type=jnp.float32
        )
        scores = scores + mask[None]
        new_max = jnp.maximum(run_max, jnp.max(scores, axis=-1))
        weights = jnp.where(mask[None] == 0.0, jnp.exp2(scores - new_max[..., None]), 0.0)
        factor = jnp.exp2(run_max - new_max)
        new_total = run_total * factor + jnp.sum(weights, axis=-1)
        new_acc = run_acc * factor[..., None] + jnp.einsum(
            "hqk,kd->hqd",
            weights.astype(jnp.bfloat16),
            block[:, size:],
            preferred_element_type=jnp.float32,
        )
        return (new_max, new_total, new_acc), None

    groups = length // chunk
    start = (
        jnp.full((heads, rows), MASKED, jnp.float32),
        jnp.zeros((heads, rows), jnp.float32),
        jnp.zeros((heads, rows, size), jnp.float32),
    )
    (_, total, acc), _ = lax.scan(
        absorb,
        start,
        (
            everything.reshape(groups, chunk, -1),
            bias.reshape(rows, groups, chunk).transpose(1, 0, 2),
        ),
    )
    out = (acc / total[..., None]).transpose(1, 0, 2).reshape(rows, width)
    return out.astype(jnp.bfloat16)


def local(
    count, sections, ring, tokens, norm_gain, query_weight, key_weight, value_weight, block_order, doc_ids
):
    rows_here = tokens[0, 0]
    row_count = rows_here.shape[0]
    length = doc_ids.shape[2]
    size = key_weight.shape[2]
    here = lax.axis_index("dp").astype(jnp.int32)[None]
    at = lax.axis_index("ctx").astype(jnp.int32)[None]
    if count != 4:
        raise ValueError("axis size")
    away = [3, 1, 2]
    weights = [key_weight[0], value_weight[0], query_weight[0]]
    slabs = cut(rows_here, here, count, away)
    arrived = {}
    for k, slab in zip(away, slabs):
        arrived[k] = swap_dp(slab, k, count)

    weight, part, *meta = prepare(
        here, rows_here, norm_gain, weights, block_order[0], doc_ids[0], ring <= DIRECT
    )
    own = to_next_section(part, 0, count, sections)
    meta = meta[0] if meta else describe_long(rows_here, block_order[0], doc_ids[0])
    meta = lax.ppermute(meta, "section", [(i, (i + 1) % sections) for i in range(sections)])
    kcos, ksin, qcos, qsin, level, bias = tables(at, meta, row_count, size, length)

    part, *halves = far_product(arrived[3], weight, size)
    kv_parts = [to_next_section(part, 3, count, sections)]
    relayed = {}
    for k, half in zip((1, 2), halves):
        relayed[3 - k] = swap_dp(half, k, count)

    q_parts = []
    for k in (1, 2):
        right = int(k == 1)
        width = query_weight.shape[2] // 2
        part = project(arrived[k], weight, [], right, 0, size)
        kv_parts.append(to_next_section(part, k, count, sections))
        part = project(arrived[k], weight, [relayed[k]], right, size, width)
        q_parts.append(to_next_section(part, k, count, sections))

    kv = mix(own, kv_parts, kcos, ksin, level)
    if ring <= DIRECT:
        pieces = [kv]
        for j in far_first(ring):
            pieces.append(swap_ctx(kv, j, ring))
        out = attend(at, own, q_parts, pieces, qcos, qsin, bias)
    else:
        everything = lax.all_gather(kv, "ctx", axis=0, tiled=True)
        out = attend_long(own, q_parts, everything, qcos, qsin, bias)
    return out[None, None]


def solution(mesh):
    in_specs = (
        P("section", "dp", "ctx", None),
        P("section", None),
        P("section", "dp", None),
        P("section", "dp", None),
        P("section", "dp", None),
        P("section", "dp", None),
        P("section", "dp", None),
    )
    out_specs = P("section", "dp", "ctx", None)

    def body(*args):
        return local(mesh.shape["dp"], mesh.shape["section"], mesh.shape["ctx"], *args)

    return jax.shard_map(body, mesh=mesh, in_specs=in_specs, out_specs=out_specs, check_vma=False)
```

```python
import functools

import jax
import jax.numpy as jnp
import numpy as np
from jax import lax
from jax.experimental import pallas as pl
from jax.experimental.pallas import tpu as pltpu
from jax.sharding import PartitionSpec as P

ROPE_BASE = 500000.0
EPSILON = 1e-05
MASKED = -1e30
LOG2E = 1.4426950408889634
DIRECT = 4
DOCS = 4
GRANT = 8 << 20


def partner(index, step, count):
    if count & (count - 1):
        raise ValueError("axis size")
    return index ^ step


def far_first(ring):
    return [3, 2, 1] if ring == 4 else list(range(ring - 1, 0, -1))


def swap_dp(x, step, count):
    return lax.ppermute(x, "dp", [(i, partner(i, step, count)) for i in range(count)])


def to_next_section(x, step, count, sections):
    moves = [
        (i * sections + s, partner(i, step, count) * sections + (s + 1) % sections)
        for i in range(count)
        for s in range(sections)
    ]
    return lax.ppermute(x, ("dp", "section"), moves)


def swap_ctx(x, step, ring):
    return lax.ppermute(x, "ctx", [(i, partner(i, step, ring)) for i in range(ring)])


def on_chip(shape, dtype):
    return pltpu.VMEM(shape, dtype)


def local_call(kernel, out_shape, args, in_specs, **more):
    in_specs = [s if isinstance(s, pl.BlockSpec) else pl.BlockSpec(memory_space=s) for s in in_specs]
    if "out_specs" not in more:
        whole = pl.BlockSpec(memory_space=pltpu.VMEM)
        more["out_specs"] = [whole] * len(out_shape) if isinstance(out_shape, list) else whole
    return pl.pallas_call(
        kernel,
        out_shape=out_shape,
        in_specs=in_specs,
        compiler_params=pltpu.CompilerParams(vmem_limit_bytes=GRANT),
        **more,
    )(*args)


def in_hbm(*arrays):
    return [pltpu.with_memory_space_constraint(x, pltpu.HBM) for x in arrays]


def cut_kernel(count, sequence, rows_ref, *refs):
    out_refs, sem = refs[:-1], refs[-1]
    here = lax.axis_index("dp")
    width = out_refs[0].shape[1]
    copies = []
    for i, k in enumerate(sequence):
        begin = pl.multiple_of(partner(here, k, count) * width, width)
        copies.append(
            pltpu.make_async_copy(rows_ref.at[:, pl.ds(begin, width)], out_refs[i], sem.at[i])
        )
    for copy in copies:
        copy.start()
    for copy in copies:
        copy.wait()


def cut(rows, count, sequence):
    height, features = rows.shape
    return local_call(
        functools.partial(cut_kernel, count, sequence),
        [on_chip((height, features // count), jnp.bfloat16)] * len(sequence),
        in_hbm(rows),
        [pltpu.HBM],
        scratch_shapes=[pltpu.SemaphoreType.DMA((len(sequence),))],
    )


def product(x, weight):
    return jnp.dot(x, weight, preferred_element_type=jnp.float32).astype(jnp.bfloat16)


def tell(rows_ref, order_ref, docs_ref, out_ref):
    height = rows_ref.shape[0]
    length, blocks = docs_ref.shape[1], order_ref.shape[1]
    block_rows = length // blocks
    squares = jnp.zeros((height, 128), jnp.float32)
    for i in range(rows_ref.shape[1] // 128):
        part = rows_ref[:, i * 128 : (i + 1) * 128].astype(jnp.float32)
        squares = squares + part * part
    mean = jnp.sum(squares, axis=1, keepdims=True) / rows_ref.shape[1]
    scale = lax.rsqrt(mean + EPSILON)
    down = lax.broadcasted_iota(jnp.int32, (height, height), 0)
    across = lax.broadcasted_iota(jnp.int32, (height, height), 1)
    out_ref[:, 2 * length :] = jnp.sum(
        jnp.where(down == across, scale, 0.0), axis=0, keepdims=True
    )
    lane = lax.broadcasted_iota(jnp.int32, (1, length), 1)
    shift = jnp.zeros((1, length), jnp.int32)
    for b in range(blocks):
        inside = (lane >= b * block_rows) & (lane < (b + 1) * block_rows)
        shift = jnp.where(inside, (order_ref[0, b] - b) * block_rows, shift)
    positions = (shift + lane).astype(jnp.float32)
    number = jnp.zeros((1, length), jnp.float32)
    for d in range(1, DOCS):
        start = jnp.sum((docs_ref[...] < d).astype(jnp.float32), axis=1, keepdims=True)
        number = number + (positions >= start).astype(jnp.float32)
    out_ref[:, :length] = positions
    out_ref[:, length : 2 * length] = number


def prepare_kernel(
    rows_hbm, gain_ref, kw_hbm, vw_hbm, qw_hbm, order_ref, docs_ref, *refs
):
    w_out, part_out = refs[:2]
    rows_ref, w_ref, sem = refs[-3:]
    half = qw_hbm.shape[1] // 2
    copies, offset = [pltpu.make_async_copy(rows_hbm, rows_ref, sem.at[0])], 0
    sources = (kw_hbm, qw_hbm.at[:, :half], vw_hbm, qw_hbm.at[:, half:])
    for i, weight in enumerate(sources):
        place = w_ref.at[:, offset : offset + weight.shape[1]]
        copies.append(pltpu.make_async_copy(weight, place, sem.at[1 + i]))
        offset += weight.shape[1]
    for copy in copies:
        copy.start()
    copies[0].wait()
    if len(refs) == 6:
        tell(rows_ref, order_ref, docs_ref, refs[2])
    width = w_out.shape[0]
    begin = pl.multiple_of(lax.axis_index("dp") * width, width)
    for copy in copies[1:]:
        copy.wait()
    step = 128
    for i in range(0, width, step):
        gain = column(gain_ref[:, pl.ds(pl.multiple_of(begin + i, step), step)])
        scaled = w_ref[i : i + step, :].astype(jnp.float32) * gain
        w_out[i : i + step, :] = scaled.astype(jnp.bfloat16)
    part_out[...] = product(rows_ref[:, pl.ds(begin, width)], w_out[...])


def prepare(rows, gain, weights, order, docs, with_meta):
    height, depth = rows.shape[0], weights[0].shape[0]
    width = sum(w.shape[1] for w in weights)
    outs = [on_chip((depth, width), jnp.bfloat16), on_chip((height, width), jnp.bfloat16)]
    if with_meta:
        outs.append(on_chip((1, 2 * docs.shape[1] + height), jnp.float32))
    return local_call(
        prepare_kernel,
        outs,
        in_hbm(rows, gain, *weights, order, docs),
        (pltpu.HBM, pltpu.VMEM, *[pltpu.HBM] * 3, pltpu.SMEM, pltpu.VMEM),
        scratch_shapes=[
            pltpu.VMEM(rows.shape, jnp.bfloat16),
            pltpu.VMEM((depth, width), jnp.bfloat16),
            pltpu.SemaphoreType.DMA((5,)),
        ],
    )


def describe_long(rows, order, docs):
    length, blocks = docs.shape[1], order.shape[1]
    wide = rows.astype(jnp.float32)
    scale = lax.rsqrt(jnp.mean(wide * wide, axis=-1) + EPSILON)
    within = jnp.arange(length // blocks, dtype=jnp.int32)
    positions = (order[0][:, None] * (length // blocks) + within[None, :]).reshape(-1)
    number = sum(
        (positions >= jnp.sum((docs[0] < d).astype(jnp.int32))).astype(jnp.float32)
        for d in range(1, DOCS)
    )
    return jnp.concatenate([positions.astype(jnp.float32), number, scale])[None]


def column(row):
    size = row.shape[1]
    down = lax.broadcasted_iota(jnp.int32, (size, size), 0)
    across = lax.broadcasted_iota(jnp.int32, (size, size), 1)
    return jnp.sum(jnp.where(down == across, row, 0.0), axis=1, keepdims=True)


def tables_kernel(length, meta_ref, kcos, ksin, qcos, qsin, level, bias):
    rows, size = kcos.shape
    begin = pl.multiple_of(lax.axis_index("ctx") * rows, rows)
    qpos = column(meta_ref[:, pl.ds(begin, rows)])
    qdoc = column(meta_ref[:, pl.ds(length + begin, rows)])
    scale = column(meta_ref[:, 2 * length :])
    lane = lax.broadcasted_iota(jnp.int32, (1, size), 1)
    pair = lax.rem(lane, size // 2).astype(jnp.float32)
    angles = qpos * jnp.exp2(pair * (-2.0 * np.log2(ROPE_BASE) / size))
    sign = jnp.where(lane < size // 2, -1.0, 1.0)
    cosine, sine = jnp.cos(angles) * scale, jnp.sin(angles) * sign * scale
    kcos[...], ksin[...] = cosine, sine
    more = size ** (-0.5) * LOG2E
    qcos[...], qsin[...] = cosine * more, sine * more
    level[...] = jnp.broadcast_to(scale, level.shape)
    allowed = (meta_ref[:, length : 2 * length] == qdoc) & (meta_ref[:, :length] <= qpos)
    bias[...] = jnp.where(allowed, 0.0, MASKED)


def tables(meta, rows, size, length):
    square = on_chip((rows, size), jnp.float32)
    return local_call(
        functools.partial(tables_kernel, length),
        [square] * 5 + [on_chip((rows, length), jnp.float32)],
        (meta,),
        (pltpu.VMEM,),
    )


def project(x, weight):
    return local_call(
        dot_kernel,
        on_chip((x.shape[0], weight.shape[1]), jnp.bfloat16),
        (x, weight),
        [pltpu.VMEM] * 2,
    )


def summed(refs, start, size):
    total = 0.0
    for ref in refs:
        total = total + ref[:, start : start + size].astype(jnp.float32)
    return total


def turn(x, cosine, sine):
    return x * cosine + pltpu.roll(x, x.shape[1] // 2, 1) * sine


def mix_kernel(own_ref, *refs):
    parts, (kcos, ksin, level, out_ref) = refs[:-4], refs[-4:]
    size, half = kcos.shape[1], own_ref.shape[1] // 2
    keys = own_ref[:, :size].astype(jnp.float32) + summed(parts, 0, size)
    values = own_ref[:, half : half + size].astype(jnp.float32) + summed(parts, size, size)
    out_ref[:, :size] = turn(keys, kcos[...], ksin[...]).astype(jnp.bfloat16)
    out_ref[:, size:] = (values * level[...]).astype(jnp.bfloat16)


def mix(own, parts, kcos, ksin, level):
    args = (own, *parts, kcos, ksin, level)
    rows, size = kcos.shape
    return local_call(
        mix_kernel, on_chip((rows, 2 * size), jnp.bfloat16), args, [pltpu.VMEM] * len(args)
    )


def far_kernel(x_ref, w_ref, kv_ref, left_ref, right_ref):
    result = product(x_ref[...], w_ref[...])
    size, half = kv_ref.shape[1] // 2, w_ref.shape[1] // 2
    kv_ref[:, :size] = result[:, :size]
    kv_ref[:, size:] = result[:, half : half + size]
    left_ref[...] = result[:, size:half]
    right_ref[...] = result[:, half + size :]


def far_product(x, weight, size):
    rows, half = x.shape[0], weight.shape[1] // 2
    outs = [on_chip((rows, w), jnp.bfloat16) for w in (2 * size, half - size, half - size)]
    return local_call(far_kernel, outs, (x, weight), [pltpu.VMEM] * 2)


def project_kernel(right, start, size, x_ref, w_ref, *refs):
    half, out_ref = w_ref.shape[1] // 2, refs[-1]
    columns = [w_ref[:, h * half + start : h * half + start + size] for h in (0, 1)]
    both = jnp.dot(
        x_ref[...], jnp.concatenate(columns, axis=1), preferred_element_type=jnp.float32
    )
    for h in (0, 1):
        part = both[:, h * size : (h + 1) * size]
        if len(refs) == 2 and h == right:
            part = part + refs[0][...].astype(jnp.float32)
        out_ref[:, h * size : (h + 1) * size] = part.astype(jnp.bfloat16)


def project(x, weight, more, right, start, size):
    return local_call(
        functools.partial(project_kernel, right, start, size),
        on_chip((x.shape[0], 2 * size), jnp.bfloat16),
        (x, weight, *more),
        [pltpu.VMEM] * (2 + len(more)),
    )


def attend_kernel(count, steps, ring, own_ref, *refs):
    at = lax.axis_index("ctx")
    parts, kv_refs = refs[:count], refs[count : count + ring]
    qcos, qsin, bias, out_ref, held, sem = refs[count + ring :]
    rows, size = qcos.shape
    heads = out_ref.shape[1] // size
    keys = jnp.concatenate([ref[:, :size] for ref in kv_refs], axis=0)
    values = jnp.concatenate([ref[:, size:] for ref in kv_refs], axis=0)
    values = jnp.concatenate([values, jnp.ones_like(values)], axis=1)
    here = [pl.multiple_of(partner(at, j, ring) * rows, rows) for j in steps]
    masks = jnp.concatenate([bias[:, pl.ds(b, rows)] for b in here], axis=1)
    copies = []
    for first in range(0, heads, 4):
        together = range(first, first + 4)
        scores, probs = {}, {}
        for h in together:
            place = own_place(h, heads, size)
            query = own_ref[:, place : place + size].astype(jnp.float32)
            query = turn(query + summed(parts, h * size, size), qcos[...], qsin[...])
            scores[h] = masks + lax.dot_general(
                query.astype(jnp.bfloat16),
                keys,
                (((1,), (1,)), ((), ())),
                preferred_element_type=jnp.float32,
            )
        for h in together:
            top = jnp.max(scores[h], axis=-1, keepdims=True)
            probs[h] = jnp.exp2(scores[h] - top).astype(jnp.bfloat16)
        for h in together:
            mixed = jnp.dot(probs[h], values, preferred_element_type=jnp.float32)
            held[h] = (mixed[:, :size] / mixed[:, size:]).astype(jnp.bfloat16)
            place = out_ref.at[:, h * size : (h + 1) * size]
            copies.append(pltpu.make_async_copy(held.at[h], place, sem.at[h]))
            copies[-1].start()
    for copy in copies:
        copy.wait()


def own_place(head, heads, size):
    return (head + (1 if head < heads // 2 else 2)) * size


def attend(own, parts, kv, qcos, qsin, bias):
    args = (own, *parts, *kv, qcos, qsin, bias)
    rows, width = parts[0].shape
    heads = width // qcos.shape[1]
    steps = [0, *far_first(len(kv))]
    return local_call(
        functools.partial(attend_kernel, len(parts), steps, len(kv)),
        jax.ShapeDtypeStruct(parts[0].shape, jnp.bfloat16),
        args,
        [pltpu.VMEM] * len(args),
        out_specs=pl.BlockSpec(memory_space=pltpu.HBM),
        scratch_shapes=[
            pltpu.VMEM((heads, rows, width // heads), jnp.bfloat16),
            pltpu.SemaphoreType.DMA((heads,)),
        ],
    )


def attend_long(own, parts, everything, qcos, qsin, bias):
    rows, width = parts[0].shape
    heads, size = width // qcos.shape[1], qcos.shape[1]
    places = [own_place(h, heads, size) for h in range(heads)]
    parts = [*parts, jnp.concatenate([own[:, p : p + size] for p in places], axis=1)]
    size = qcos.shape[1]
    heads = width // size
    total_q = sum(p.astype(jnp.float32) for p in parts).reshape(rows, heads, size)
    turned = jnp.concatenate([total_q[..., size // 2 :], total_q[..., : size // 2]], axis=-1)
    queries = (total_q * qcos[:, None] + turned * qsin[:, None]).astype(jnp.bfloat16)
    length = everything.shape[0]
    chunk = 1024 if length % 1024 == 0 else length

    def absorb(state, piece):
        run_max, run_total, run_acc = state
        block, mask = piece
        scores = jnp.einsum(
            "qhd,kd->hqk", queries, block[:, :size], preferred_element_type=jnp.float32
        )
        scores = scores + mask[None]
        new_max = jnp.maximum(run_max, jnp.max(scores, axis=-1))
        weights = jnp.where(mask[None] == 0.0, jnp.exp2(scores - new_max[..., None]), 0.0)
        factor = jnp.exp2(run_max - new_max)
        new_total = run_total * factor + jnp.sum(weights, axis=-1)
        new_acc = run_acc * factor[..., None] + jnp.einsum(
            "hqk,kd->hqd",
            weights.astype(jnp.bfloat16),
            block[:, size:],
            preferred_element_type=jnp.float32,
        )
        return (new_max, new_total, new_acc), None

    groups = length // chunk
    start = (
        jnp.full((heads, rows), MASKED, jnp.float32),
        jnp.zeros((heads, rows), jnp.float32),
        jnp.zeros((heads, rows, size), jnp.float32),
    )
    (_, total, acc), _ = lax.scan(
        absorb,
        start,
        (
            everything.reshape(groups, chunk, -1),
            bias.reshape(rows, groups, chunk).transpose(1, 0, 2),
        ),
    )
    out = (acc / total[..., None]).transpose(1, 0, 2).reshape(rows, width)
    return out.astype(jnp.bfloat16)


def local(
    count, sections, ring, tokens, norm_gain, query_weight, key_weight, value_weight, block_order, doc_ids
):
    rows_here = tokens[0, 0]
    row_count = rows_here.shape[0]
    length = doc_ids.shape[2]
    size = key_weight.shape[2]
    if count != 4:
        raise ValueError("axis size")
    away = [3, 2, 1]
    weights = [key_weight[0], value_weight[0], query_weight[0]]
    slabs = cut(rows_here, count, away)
    arrived = {}
    for k, slab in zip(away, slabs):
        arrived[k] = swap_dp(slab, k, count)

    weight, part, *meta = prepare(
        rows_here, norm_gain, weights, block_order[0], doc_ids[0], ring <= DIRECT
    )
    own = to_next_section(part, 0, count, sections)
    meta = meta[0] if meta else describe_long(rows_here, block_order[0], doc_ids[0])
    meta = lax.ppermute(meta, "section", [(i, (i + 1) % sections) for i in range(sections)])
    kcos, ksin, qcos, qsin, level, bias = tables(meta, row_count, size, length)

    part, *halves = far_product(arrived[3], weight, size)
    kv_parts = [to_next_section(part, 3, count, sections)]
    relayed = {}
    for k, half in zip((1, 2), halves):
        relayed[3 - k] = swap_dp(half, k, count)

    q_parts = []
    for k in (1, 2):
        right = int(k == 1)
        width = query_weight.shape[2] // 2
        part = project(arrived[k], weight, [], right, 0, size)
        kv_parts.append(to_next_section(part, k, count, sections))
        part = project(arrived[k], weight, [relayed[k]], right, size, width)
        q_parts.append(to_next_section(part, k, count, sections))

    kv = mix(own, kv_parts, kcos, ksin, level)
    if ring <= DIRECT:
        pieces = [kv]
        for j in far_first(ring):
            pieces.append(swap_ctx(kv, j, ring))
        out = attend(own, q_parts, pieces, qcos, qsin, bias)
    else:
        everything = lax.all_gather(kv, "ctx", axis=0, tiled=True)
        out = attend_long(own, q_parts, everything, qcos, qsin, bias)
    return out[None, None]


def solution(mesh):
    in_specs = (
        P("section", "dp", "ctx", None),
        P("section", None),
        P("section", "dp", None),
        P("section", "dp", None),
        P("section", "dp", None),
        P("section", "dp", None),
        P("section", "dp", None),
    )
    out_specs = P("section", "dp", "ctx", None)

    def body(*args):
        return local(mesh.shape["dp"], mesh.shape["section"], mesh.shape["ctx"], *args)

    return jax.shard_map(body, mesh=mesh, in_specs=in_specs, out_specs=out_specs, check_vma=False)
```

```python
import functools

import jax
import jax.numpy as jnp
import numpy as np
from jax import lax
from jax.experimental import pallas as pl
from jax.experimental.pallas import tpu as pltpu
from jax.sharding import PartitionSpec as P

ROPE_BASE = 500000.0
EPSILON = 1e-05
MASKED = -1e30
LOG2E = 1.4426950408889634
DIRECT = 4
DOCS = 4
GRANT = 8 << 20


def partner(index, step, count):
    if count & (count - 1):
        raise ValueError("axis size")
    return index ^ step


def far_first(ring):
    return [3, 2, 1] if ring == 4 else list(range(ring - 1, 0, -1))


def swap_dp(x, step, count):
    return lax.ppermute(x, "dp", [(i, partner(i, step, count)) for i in range(count)])


def to_next_section(x, step, count, sections):
    moves = [
        (i * sections + s, partner(i, step, count) * sections + (s + 1) % sections)
        for i in range(count)
        for s in range(sections)
    ]
    return lax.ppermute(x, ("dp", "section"), moves)


def swap_ctx(x, step, ring):
    return lax.ppermute(x, "ctx", [(i, partner(i, step, ring)) for i in range(ring)])


def on_chip(shape, dtype):
    return pltpu.VMEM(shape, dtype)


def local_call(kernel, out_shape, args, in_specs, **more):
    in_specs = [s if isinstance(s, pl.BlockSpec) else pl.BlockSpec(memory_space=s) for s in in_specs]
    if "out_specs" not in more:
        whole = pl.BlockSpec(memory_space=pltpu.VMEM)
        more["out_specs"] = [whole] * len(out_shape) if isinstance(out_shape, list) else whole
    return pl.pallas_call(
        kernel,
        out_shape=out_shape,
        in_specs=in_specs,
        compiler_params=pltpu.CompilerParams(vmem_limit_bytes=GRANT),
        **more,
    )(*args)


def in_hbm(*arrays):
    return [pltpu.with_memory_space_constraint(x, pltpu.HBM) for x in arrays]


def cut_kernel(count, sequence, rows_ref, *refs):
    out_refs, sem = refs[:-1], refs[-1]
    here = lax.axis_index("dp")
    width = out_refs[0].shape[1]
    copies = []
    for i, k in enumerate(sequence):
        begin = pl.multiple_of(partner(here, k, count) * width, width)
        copies.append(
            pltpu.make_async_copy(rows_ref.at[:, pl.ds(begin, width)], out_refs[i], sem.at[i])
        )
    for copy in copies:
        copy.start()
    for copy in copies:
        copy.wait()


def cut(rows, count, sequence):
    height, features = rows.shape
    return local_call(
        functools.partial(cut_kernel, count, sequence),
        [on_chip((height, features // count), jnp.bfloat16)] * len(sequence),
        in_hbm(rows),
        [pltpu.HBM],
        scratch_shapes=[pltpu.SemaphoreType.DMA((len(sequence),))],
    )


def product(x, weight):
    return jnp.dot(x, weight, preferred_element_type=jnp.float32).astype(jnp.bfloat16)


def tell(rows_ref, order_ref, docs_ref, out_ref):
    height = rows_ref.shape[0]
    length, blocks = docs_ref.shape[1], order_ref.shape[1]
    block_rows = length // blocks
    squares = jnp.zeros((height, 128), jnp.float32)
    for i in range(rows_ref.shape[1] // 128):
        part = rows_ref[:, i * 128 : (i + 1) * 128].astype(jnp.float32)
        squares = squares + part * part
    mean = jnp.sum(squares, axis=1, keepdims=True) / rows_ref.shape[1]
    scale = lax.rsqrt(mean + EPSILON)
    down = lax.broadcasted_iota(jnp.int32, (height, height), 0)
    across = lax.broadcasted_iota(jnp.int32, (height, height), 1)
    out_ref[:, 2 * length :] = jnp.sum(
        jnp.where(down == across, scale, 0.0), axis=0, keepdims=True
    )
    lane = lax.broadcasted_iota(jnp.int32, (1, length), 1)
    shift = jnp.zeros((1, length), jnp.int32)
    for b in range(blocks):
        inside = (lane >= b * block_rows) & (lane < (b + 1) * block_rows)
        shift = jnp.where(inside, (order_ref[0, b] - b) * block_rows, shift)
    positions = (shift + lane).astype(jnp.float32)
    number = jnp.zeros((1, length), jnp.float32)
    for d in range(1, DOCS):
        start = jnp.sum((docs_ref[...] < d).astype(jnp.float32), axis=1, keepdims=True)
        number = number + (positions >= start).astype(jnp.float32)
    out_ref[:, :length] = positions
    out_ref[:, length : 2 * length] = number


def prepare_kernel(
    rows_hbm, gain_ref, kw_hbm, vw_hbm, qw_hbm, order_ref, docs_ref, *refs
):
    w_out, part_out = refs[:2]
    rows_ref, w_ref, sem = refs[-3:]
    half = qw_hbm.shape[1] // 2
    copies, offset = [pltpu.make_async_copy(rows_hbm, rows_ref, sem.at[0])], 0
    sources = (kw_hbm, qw_hbm.at[:, :half], vw_hbm, qw_hbm.at[:, half:])
    for i, weight in enumerate(sources):
        place = w_ref.at[:, offset : offset + weight.shape[1]]
        copies.append(pltpu.make_async_copy(weight, place, sem.at[1 + i]))
        offset += weight.shape[1]
    for copy in copies:
        copy.start()
    copies[0].wait()
    if len(refs) == 6:
        tell(rows_ref, order_ref, docs_ref, refs[2])
    width = w_out.shape[0]
    begin = pl.multiple_of(lax.axis_index("dp") * width, width)
    for copy in copies[1:]:
        copy.wait()
    step = 128
    for i in range(0, width, step):
        gain = column(gain_ref[:, pl.ds(pl.multiple_of(begin + i, step), step)])
        scaled = w_ref[i : i + step, :].astype(jnp.float32) * gain
        w_out[i : i + step, :] = scaled.astype(jnp.bfloat16)
    part_out[...] = product(rows_ref[:, pl.ds(begin, width)], w_out[...])


def prepare(rows, gain, weights, order, docs, with_meta):
    height, depth = rows.shape[0], weights[0].shape[0]
    width = sum(w.shape[1] for w in weights)
    outs = [on_chip((depth, width), jnp.bfloat16), on_chip((height, width), jnp.bfloat16)]
    if with_meta:
        outs.append(on_chip((1, 2 * docs.shape[1] + height), jnp.float32))
    return local_call(
        prepare_kernel,
        outs,
        in_hbm(rows, gain, *weights, order, docs),
        (pltpu.HBM, pltpu.VMEM, *[pltpu.HBM] * 3, pltpu.SMEM, pltpu.VMEM),
        scratch_shapes=[
            pltpu.VMEM(rows.shape, jnp.bfloat16),
            pltpu.VMEM((depth, width), jnp.bfloat16),
            pltpu.SemaphoreType.DMA((5,)),
        ],
    )


def describe_long(rows, order, docs):
    length, blocks = docs.shape[1], order.shape[1]
    wide = rows.astype(jnp.float32)
    scale = lax.rsqrt(jnp.mean(wide * wide, axis=-1) + EPSILON)
    within = jnp.arange(length // blocks, dtype=jnp.int32)
    positions = (order[0][:, None] * (length // blocks) + within[None, :]).reshape(-1)
    number = sum(
        (positions >= jnp.sum((docs[0] < d).astype(jnp.int32))).astype(jnp.float32)
        for d in range(1, DOCS)
    )
    return jnp.concatenate([positions.astype(jnp.float32), number, scale])[None]


def column(row):
    size = row.shape[1]
    down = lax.broadcasted_iota(jnp.int32, (size, size), 0)
    across = lax.broadcasted_iota(jnp.int32, (size, size), 1)
    return jnp.sum(jnp.where(down == across, row, 0.0), axis=1, keepdims=True)


def tables_kernel(length, meta_ref, kcos, ksin, qcos, qsin, level, bias):
    rows, size = kcos.shape
    begin = pl.multiple_of(lax.axis_index("ctx") * rows, rows)
    qpos = column(meta_ref[:, pl.ds(begin, rows)])
    qdoc = column(meta_ref[:, pl.ds(length + begin, rows)])
    scale = column(meta_ref[:, 2 * length :])
    lane = lax.broadcasted_iota(jnp.int32, (1, size), 1)
    pair = lax.rem(lane, size // 2).astype(jnp.float32)
    angles = qpos * jnp.exp2(pair * (-2.0 * np.log2(ROPE_BASE) / size))
    sign = jnp.where(lane < size // 2, -1.0, 1.0)
    cosine, sine = jnp.cos(angles) * scale, jnp.sin(angles) * sign * scale
    kcos[...], ksin[...] = cosine, sine
    more = size ** (-0.5) * LOG2E
    qcos[...], qsin[...] = cosine * more, sine * more
    level[...] = jnp.broadcast_to(scale, level.shape)
    allowed = (meta_ref[:, length : 2 * length] == qdoc) & (meta_ref[:, :length] <= qpos)
    bias[...] = jnp.where(allowed, 0.0, MASKED)


def tables(meta, rows, size, length):
    square = on_chip((rows, size), jnp.float32)
    return local_call(
        functools.partial(tables_kernel, length),
        [square] * 5 + [on_chip((rows, length), jnp.float32)],
        (meta,),
        (pltpu.VMEM,),
    )


def summed(refs, start, size):
    total = 0.0
    for ref in refs:
        total = total + ref[:, start : start + size].astype(jnp.float32)
    return total


def turn(x, cosine, sine):
    return x * cosine + pltpu.roll(x, x.shape[1] // 2, 1) * sine


def mix_kernel(own_ref, *refs):
    parts, (kcos, ksin, level, out_ref) = refs[:-4], refs[-4:]
    size, half = kcos.shape[1], own_ref.shape[1] // 2
    keys = own_ref[:, :size].astype(jnp.float32) + summed(parts, 0, size)
    values = own_ref[:, half : half + size].astype(jnp.float32) + summed(parts, size, size)
    out_ref[:, :size] = turn(keys, kcos[...], ksin[...]).astype(jnp.bfloat16)
    out_ref[:, size:] = (values * level[...]).astype(jnp.bfloat16)


def mix(own, parts, kcos, ksin, level):
    args = (own, *parts, kcos, ksin, level)
    rows, size = kcos.shape
    return local_call(
        mix_kernel, on_chip((rows, 2 * size), jnp.bfloat16), args, [pltpu.VMEM] * len(args)
    )


def far_kernel(x_ref, w_ref, kv_ref, left_ref, right_ref):
    result = product(x_ref[...], w_ref[...])
    size, half = kv_ref.shape[1] // 2, w_ref.shape[1] // 2
    kv_ref[:, :size] = result[:, :size]
    kv_ref[:, size:] = result[:, half : half + size]
    left_ref[...] = result[:, size:half]
    right_ref[...] = result[:, half + size :]


def far_product(x, weight, size):
    rows, half = x.shape[0], weight.shape[1] // 2
    outs = [on_chip((rows, w), jnp.bfloat16) for w in (2 * size, half - size, half - size)]
    return local_call(far_kernel, outs, (x, weight), [pltpu.VMEM] * 2)


def project_kernel(right, start, size, x_ref, w_ref, *refs):
    half, out_ref = w_ref.shape[1] // 2, refs[-1]
    columns = [w_ref[:, h * half + start : h * half + start + size] for h in (0, 1)]
    both = jnp.dot(
        x_ref[...], jnp.concatenate(columns, axis=1), preferred_element_type=jnp.float32
    )
    for h in (0, 1):
        part = both[:, h * size : (h + 1) * size]
        if len(refs) == 2 and h == right:
            part = part + refs[0][...].astype(jnp.float32)
        out_ref[:, h * size : (h + 1) * size] = part.astype(jnp.bfloat16)


def project(x, weight, more, right, start, size):
    return local_call(
        functools.partial(project_kernel, right, start, size),
        on_chip((x.shape[0], 2 * size), jnp.bfloat16),
        (x, weight, *more),
        [pltpu.VMEM] * (2 + len(more)),
    )


def attend_kernel(count, steps, ring, own_ref, *refs):
    at = lax.axis_index("ctx")
    parts, kv_refs = refs[:count], refs[count : count + ring]
    qcos, qsin, bias, out_ref, held, sem = refs[count + ring :]
    rows, size = qcos.shape
    heads = out_ref.shape[1] // size
    keys = jnp.concatenate([ref[:, :size] for ref in kv_refs], axis=0)
    values = jnp.concatenate([ref[:, size:] for ref in kv_refs], axis=0)
    values = jnp.concatenate([values, jnp.ones_like(values)], axis=1)
    here = [pl.multiple_of(partner(at, j, ring) * rows, rows) for j in steps]
    masks = jnp.concatenate([bias[:, pl.ds(b, rows)] for b in here], axis=1)
    copies = []
    for first in range(0, heads, 4):
        together = range(first, first + 4)
        scores, probs = {}, {}
        for h in together:
            place = own_place(h, heads, size)
            query = own_ref[:, place : place + size].astype(jnp.float32)
            query = turn(query + summed(parts, h * size, size), qcos[...], qsin[...])
            scores[h] = masks + lax.dot_general(
                query.astype(jnp.bfloat16),
                keys,
                (((1,), (1,)), ((), ())),
                preferred_element_type=jnp.float32,
            )
        for h in together:
            top = jnp.max(scores[h], axis=-1, keepdims=True)
            probs[h] = jnp.exp2(scores[h] - top).astype(jnp.bfloat16)
        for h in together:
            mixed = jnp.dot(probs[h], values, preferred_element_type=jnp.float32)
            held[h] = (mixed[:, :size] / mixed[:, size:]).astype(jnp.bfloat16)
            place = out_ref.at[:, h * size : (h + 1) * size]
            copies.append(pltpu.make_async_copy(held.at[h], place, sem.at[h]))
            copies[-1].start()
    for copy in copies:
        copy.wait()


def own_place(head, heads, size):
    return (head + (1 if head < heads // 2 else 2)) * size


def attend(own, parts, kv, qcos, qsin, bias):
    args = (own, *parts, *kv, qcos, qsin, bias)
    rows, width = parts[0].shape
    heads = width // qcos.shape[1]
    steps = [0, *far_first(len(kv))]
    return local_call(
        functools.partial(attend_kernel, len(parts), steps, len(kv)),
        jax.ShapeDtypeStruct(parts[0].shape, jnp.bfloat16),
        args,
        [pltpu.VMEM] * len(args),
        out_specs=pl.BlockSpec(memory_space=pltpu.HBM),
        scratch_shapes=[
            pltpu.VMEM((heads, rows, width // heads), jnp.bfloat16),
            pltpu.SemaphoreType.DMA((heads,)),
        ],
    )


def attend_long(own, parts, everything, qcos, qsin, bias):
    rows, width = parts[0].shape
    heads, size = width // qcos.shape[1], qcos.shape[1]
    places = [own_place(h, heads, size) for h in range(heads)]
    parts = [*parts, jnp.concatenate([own[:, p : p + size] for p in places], axis=1)]
    size = qcos.shape[1]
    heads = width // size
    total_q = sum(p.astype(jnp.float32) for p in parts).reshape(rows, heads, size)
    turned = jnp.concatenate([total_q[..., size // 2 :], total_q[..., : size // 2]], axis=-1)
    queries = (total_q * qcos[:, None] + turned * qsin[:, None]).astype(jnp.bfloat16)
    length = everything.shape[0]
    chunk = 1024 if length % 1024 == 0 else length

    def absorb(state, piece):
        run_max, run_total, run_acc = state
        block, mask = piece
        scores = jnp.einsum(
            "qhd,kd->hqk", queries, block[:, :size], preferred_element_type=jnp.float32
        )
        scores = scores + mask[None]
        new_max = jnp.maximum(run_max, jnp.max(scores, axis=-1))
        weights = jnp.where(mask[None] == 0.0, jnp.exp2(scores - new_max[..., None]), 0.0)
        factor = jnp.exp2(run_max - new_max)
        new_total = run_total * factor + jnp.sum(weights, axis=-1)
        new_acc = run_acc * factor[..., None] + jnp.einsum(
            "hqk,kd->hqd",
            weights.astype(jnp.bfloat16),
            block[:, size:],
            preferred_element_type=jnp.float32,
        )
        return (new_max, new_total, new_acc), None

    groups = length // chunk
    start = (
        jnp.full((heads, rows), MASKED, jnp.float32),
        jnp.zeros((heads, rows), jnp.float32),
        jnp.zeros((heads, rows, size), jnp.float32),
    )
    (_, total, acc), _ = lax.scan(
        absorb,
        start,
        (
            everything.reshape(groups, chunk, -1),
            bias.reshape(rows, groups, chunk).transpose(1, 0, 2),
        ),
    )
    out = (acc / total[..., None]).transpose(1, 0, 2).reshape(rows, width)
    return out.astype(jnp.bfloat16)


def local(
    count, sections, ring, tokens, norm_gain, query_weight, key_weight, value_weight, block_order, doc_ids
):
    rows_here = tokens[0, 0]
    row_count = rows_here.shape[0]
    length = doc_ids.shape[2]
    size = key_weight.shape[2]
    if count != 4:
        raise ValueError("axis size")
    away = [3, 2, 1]
    weights = [key_weight[0], value_weight[0], query_weight[0]]
    slabs = list(cut(rows_here, count, away[:1]))
    slabs += cut(rows_here, count, away[1:])
    arrived = {}
    for k, slab in zip(away, slabs):
        arrived[k] = swap_dp(slab, k, count)

    weight, part, *meta = prepare(
        rows_here, norm_gain, weights, block_order[0], doc_ids[0], ring <= DIRECT
    )
    own = to_next_section(part, 0, count, sections)
    meta = meta[0] if meta else describe_long(rows_here, block_order[0], doc_ids[0])
    meta = lax.ppermute(meta, "section", [(i, (i + 1) % sections) for i in range(sections)])
    kcos, ksin, qcos, qsin, level, bias = tables(meta, row_count, size, length)

    part, *halves = far_product(arrived[3], weight, size)
    kv_parts = [to_next_section(part, 3, count, sections)]
    relayed = {}
    for k, half in zip((1, 2), halves):
        relayed[3 - k] = swap_dp(half, k, count)

    q_parts = []
    for k in (1, 2):
        right = int(k == 1)
        width = query_weight.shape[2] // 2
        part = project(arrived[k], weight, [], right, 0, size)
        kv_parts.append(to_next_section(part, k, count, sections))
        part = project(arrived[k], weight, [relayed[k]], right, size, width)
        q_parts.append(to_next_section(part, k, count, sections))

    kv = mix(own, kv_parts, kcos, ksin, level)
    if ring <= DIRECT:
        pieces = [kv]
        for j in far_first(ring):
            pieces.append(swap_ctx(kv, j, ring))
        out = attend(own, q_parts, pieces, qcos, qsin, bias)
    else:
        everything = lax.all_gather(kv, "ctx", axis=0, tiled=True)
        out = attend_long(own, q_parts, everything, qcos, qsin, bias)
    return out[None, None]


def solution(mesh):
    in_specs = (
        P("section", "dp", "ctx", None),
        P("section", None),
        P("section", "dp", None),
        P("section", "dp", None),
        P("section", "dp", None),
        P("section", "dp", None),
        P("section", "dp", None),
    )
    out_specs = P("section", "dp", "ctx", None)

    def body(*args):
        return local(mesh.shape["dp"], mesh.shape["section"], mesh.shape["ctx"], *args)

    return jax.shard_map(body, mesh=mesh, in_specs=in_specs, out_specs=out_specs, check_vma=False)
```
